32 devices in a mesh: dp: 4 (over x, core), ctx: 4 (over z), rep: 2 (over y).
Axes of the slice: x: 2, y: 2, z: 4, core: 2. Of those that a mesh axis runs over, the one named last changes fastest.
Arguments:
- tokens: bfloat16 [8, 1024, 576], P(('dp', 'rep'), 'ctx'), may hold values from -6 to 6
- out_grad: bfloat16 [8, 1024, 576], P(('dp', 'rep'), 'ctx'), may hold values from -6 to 6
- segments: int32 [8, 1024], P(('dp', 'rep')), may hold values from 0 to 3, never falling along the last dimension, each value on 1 to 512 neighbouring positions
- query_copy: bfloat16 [576, 576], P(('dp', 'ctx')), may hold values from -0.25 to 0.25
- key_copy: bfloat16 [576, 192], P(('dp', 'ctx')), may hold values from -0.25 to 0.25
- value_copy: bfloat16 [576, 192], P(('dp', 'ctx')), may hold values from -0.25 to 0.25
- output_copy: bfloat16 [576, 576], P(('dp', 'ctx')), may hold values from -0.75 to 0.75
- gate_copy: bfloat16 [576, 1536], P(None, ('dp', 'ctx')), may hold values from -0.25 to 0.25
- up_copy: bfloat16 [576, 1536], P(None, ('dp', 'ctx')), may hold values from -0.25 to 0.25
- down_copy: bfloat16 [1536, 576], P(('dp', 'ctx')), may hold values from -0.15625 to 0.15625
- gains_copy: bfloat16 [2, 576], P(None, ('dp', 'ctx')), may hold values from 0.5 to 1.5
- query_master: float32 [576, 576], P(('dp', 'ctx')), may hold values from -0.25 to 0.25
- key_master: float32 [576, 192], P(('dp', 'ctx')), may hold values from -0.25 to 0.25
- value_master: float32 [576, 192], P(('dp', 'ctx')), may hold values from -0.25 to 0.25
- output_master: float32 [576, 576], P(('dp', 'ctx')), may hold values from -0.75 to 0.75
- gate_master: float32 [576, 1536], P(None, ('dp', 'ctx')), may hold values from -0.25 to 0.25
- up_master: float32 [576, 1536], P(None, ('dp', 'ctx')), may hold values from -0.25 to 0.25
- down_master: float32 [1536, 576], P(('dp', 'ctx')), may hold values from -0.15625 to 0.15625
- gains_master: float32 [2, 576], P(None, ('dp', 'ctx')), may hold values from 0.5 to 1.5
- query_moment: float32 [576, 576], P(('dp', 'ctx')), may hold values from -160 to 160
- key_moment: float32 [576, 192], P(('dp', 'ctx')), may hold values from -160 to 160
- value_moment: float32 [576, 192], P(('dp', 'ctx')), may hold values from -56 to 56
- output_moment: float32 [576, 576], P(('dp', 'ctx')), may hold values from -56 to 56
- gate_moment: float32 [576, 1536], P(None, ('dp', 'ctx')), may hold values from -160 to 160
- up_moment: float32 [576, 1536], P(None, ('dp', 'ctx')), may hold values from -160 to 160
- down_moment: float32 [1536, 576], P(('dp', 'ctx')), may hold values from -160 to 160
- gains_moment: float32 [2, 576], P(None, ('dp', 'ctx')), may hold values from -160 to 160
Outputs:
- out_tokens: bfloat16 [8, 1024, 576], P(('dp', 'rep'), 'ctx')
- in_grad: float32 [8, 1024, 576], P(('dp', 'rep'), 'ctx')
- query_grad: float32 [576, 576], P(('dp', 'ctx'))
- key_grad: float32 [576, 192], P(('dp', 'ctx'))
- value_grad: float32 [576, 192], P(('dp', 'ctx'))
- output_grad: float32 [576, 576], P(('dp', 'ctx'))
- gate_grad: float32 [576, 1536], P(None, ('dp', 'ctx'))
- up_grad: float32 [576, 1536], P(None, ('dp', 'ctx'))
- down_grad: float32 [1536, 576], P(('dp', 'ctx'))
- gains_grad: float32 [2, 576], P(None, ('dp', 'ctx'))
- query_momentum: float32 [576, 576], P(('dp', 'ctx'))
- key_momentum: float32 [576, 192], P(('dp', 'ctx'))
- value_momentum: float32 [576, 192], P(('dp', 'ctx'))
- output_momentum: float32 [576, 576], P(('dp', 'ctx'))
- gate_momentum: float32 [576, 1536], P(None, ('dp', 'ctx'))
- up_momentum: float32 [576, 1536], P(None, ('dp', 'ctx'))
- down_momentum: float32 [1536, 576], P(('dp', 'ctx'))
- gains_momentum: float32 [2, 576], P(None, ('dp', 'ctx'))
- query_weight: float32 [576, 576], P(('dp', 'ctx'))
- key_weight: float32 [576, 192], P(('dp', 'ctx'))
- value_weight: float32 [576, 192], P(('dp', 'ctx'))
- output_weight: float32 [576, 576], P(('dp', 'ctx'))
- gate_weight: float32 [576, 1536], P(None, ('dp', 'ctx'))
- up_weight: float32 [576, 1536], P(None, ('dp', 'ctx'))
- down_weight: float32 [1536, 576], P(('dp', 'ctx'))
- gains_weight: float32 [2, 576], P(None, ('dp', 'ctx'))
- query_rounded: bfloat16 [576, 576], P(('dp', 'ctx'))
- key_rounded: bfloat16 [576, 192], P(('dp', 'ctx'))
- value_rounded: bfloat16 [576, 192], P(('dp', 'ctx'))
- output_rounded: bfloat16 [576, 576], P(('dp', 'ctx'))
- gate_rounded: bfloat16 [576, 1536], P(None, ('dp', 'ctx'))
- up_rounded: bfloat16 [576, 1536], P(None, ('dp', 'ctx'))
- down_rounded: bfloat16 [1536, 576], P(('dp', 'ctx'))
- gains_rounded: bfloat16 [2, 576], P(None, ('dp', 'ctx'))
The draws below stay inside these ranges and needn't reach their ends.
Inputs may be any that keep to these rules, and one draw needn't show every extreme that they name: `segments`: in each sequence the document numbers never fall; each number from 0 to 3 covers 1 to 512 consecutive tokens, and one covers exactly 512.
All inputs are finite; a program needn't handle non-finite values.
Results may differ from the reference program's by a relative error of at most 0.018.
Values may be sent and summed in bfloat16 or wider, within the bound.
No kernel may reach another device: no remote copies, remote signals or barrier semaphores. Data moves between devices by JAX's collectives and lax.ppermute only.
A program may use at most 192 MiB of HBM per device.

```python
import math
import jax
import jax.numpy as jnp
import numpy as np
from jax import lax

D = 576
H = 9
KVH = 3
HD = 64
FF = 1536
NS_STEPS = 5
QW = 576
KVW = 192
LEN = 1024
SEQS = 8
DOCS = 4
DOC_MAX = 512


def block_levels(key, shape, pieces, smallest, high):
    def one(position, blocks):
        steps = jax.random.uniform(jax.random.fold_in(jax.random.fold_in(key, 6), position), (blocks,), jnp.float32, smallest / len(pieces), high / len(pieces))
        return jnp.repeat(jnp.exp(steps), shape[position] // blocks).reshape((-1,) + (1,) * (len(shape) - position - 1))

    gain = one(*pieces[0])
    for cut in pieces[1:]:
        gain = gain * one(*cut)
    return gain


def profile(count, total, bound, lean):
    portions = [(1 << 20) // math.isqrt(standing ** lean) + 1 for standing in range(2, count + 1)]
    surplus, given = total - bound - (count - 1), [1] * (count - 1)
    while surplus > 0:
        movable = [i for i in range(count - 1) if given[i] < bound]
        mass, left = sum([portions[i] for i in movable]), surplus
        for i in movable:
            more = min(bound - given[i], max(1, left * portions[i] // mass), surplus)
            given[i] = given[i] + more
            surplus = surplus - more
    return np.array([bound] + given)


def ragged(stream_key, number_of, total, reach, lean):
    if number_of == 2:
        one = jax.random.randint(stream_key, (), max(1, total - reach), min(reach, total - 1) + 1)
        return jnp.stack([one, total - one])
    sizes = jnp.asarray(profile(number_of, total, reach, lean), jnp.int32)
    couples = (number_of - 1) // 2
    donor, receiver = sizes[1:1 + 2 * couples:2], sizes[2:2 + 2 * couples:2]
    room = jnp.minimum(donor - 1, reach - receiver)
    shifted = jax.random.randint(jax.random.fold_in(stream_key, 1), (couples,), 0, 1 << 20) % (room + 1)
    sizes = sizes.at[1:1 + 2 * couples:2].set(donor - shifted).at[2:2 + 2 * couples:2].set(receiver + shifted)
    return sizes[jax.random.permutation(jax.random.fold_in(stream_key, 2), number_of)]


def centred(rng, dims, deviation, limit, split=(), held_as=jnp.bfloat16):
    values = deviation * jax.random.normal(rng, dims, jnp.float32)
    if split:
        values = values * block_levels(rng, dims, split, -0.22, 0.18)
    return jnp.clip(values, -limit, limit).astype(held_as)


def setup_inputs(seed: int = 0) -> dict:
    key_list = jax.random.split(jax.random.key(seed), 28)
    return {
        "tokens": centred(key_list[0], (SEQS, LEN, D), 1.0, 6.0, ((0, 8), (1, 4))),
        "out_grad": centred(key_list[1], (SEQS, LEN, D), 1.0, 6.0, ((0, 8), (1, 4))),
        "segments": jax.vmap(lambda own: jnp.searchsorted(jnp.cumsum(ragged(own, DOCS, LEN, DOC_MAX, 2)), jnp.arange(LEN), side="right"))(jax.random.split(key_list[2], SEQS)).reshape((SEQS, LEN)).astype(jnp.int32),
        "query_copy": centred(key_list[3], (D, QW), D ** -0.5, 0.25, ((0, 16),)),
        "key_copy": centred(key_list[4], (D, KVW), D ** -0.5, 0.25, ((0, 16),)),
        "value_copy": centred(key_list[5], (D, KVW), D ** -0.5, 0.25, ((0, 16),)),
        "output_copy": centred(key_list[6], (QW, D), HD ** -0.5, 0.75, ((0, 16),)),
        "gate_copy": centred(key_list[7], (D, FF), D ** -0.5, 0.25, ((1, 16),)),
        "up_copy": centred(key_list[8], (D, FF), D ** -0.5, 0.25, ((1, 16),)),
        "down_copy": centred(key_list[9], (FF, D), FF ** -0.5, 0.15625, ((0, 16),)),
        "gains_copy": jnp.clip(1.0 + 0.1 * jax.random.normal(key_list[10], (2, D), jnp.float32), 0.5, 1.5).astype(jnp.bfloat16),
        "query_master": centred(key_list[11], (D, QW), D ** -0.5, 0.25, ((0, 16),), jnp.float32),
        "key_master": centred(key_list[12], (D, KVW), D ** -0.5, 0.25, ((0, 16),), jnp.float32),
        "value_master": centred(key_list[13], (D, KVW), D ** -0.5, 0.25, ((0, 16),), jnp.float32),
        "output_master": centred(key_list[14], (QW, D), HD ** -0.5, 0.75, ((0, 16),), jnp.float32),
        "gate_master": centred(key_list[15], (D, FF), D ** -0.5, 0.25, ((1, 16),), jnp.float32),
        "up_master": centred(key_list[16], (D, FF), D ** -0.5, 0.25, ((1, 16),), jnp.float32),
        "down_master": centred(key_list[17], (FF, D), FF ** -0.5, 0.15625, ((0, 16),), jnp.float32),
        "gains_master": jnp.clip(1.0 + 0.1 * jax.random.normal(key_list[18], (2, D), jnp.float32), 0.5, 1.5),
        "query_moment": centred(key_list[19], (D, QW), (0.3 * (SEQS * LEN) ** 0.5), 160.0, ((0, 16),), jnp.float32),
        "key_moment": centred(key_list[20], (D, KVW), (0.3 * (SEQS * LEN) ** 0.5), 160.0, ((0, 16),), jnp.float32),
        "value_moment": centred(key_list[21], (D, KVW), (0.1 * (SEQS * LEN) ** 0.5), 56.0, ((0, 16),), jnp.float32),
        "output_moment": centred(key_list[22], (QW, D), (0.1 * (SEQS * LEN) ** 0.5), 56.0, ((0, 16),), jnp.float32),
        "gate_moment": centred(key_list[23], (D, FF), (0.3 * (SEQS * LEN) ** 0.5), 160.0, ((1, 16),), jnp.float32),
        "up_moment": centred(key_list[24], (D, FF), (0.3 * (SEQS * LEN) ** 0.5), 160.0, ((1, 16),), jnp.float32),
        "down_moment": centred(key_list[25], (FF, D), (0.3 * (SEQS * LEN) ** 0.5), 160.0, ((0, 16),), jnp.float32),
        "gains_moment": centred(key_list[26], (2, D), (0.3 * (SEQS * LEN) ** 0.5), 160.0, ((1, 16),), jnp.float32),
    }


EPSILON = 1e-05
ROPE_BASE = 10000.0
MASKED_SCORE = -1e+30
MOMENTUM = 0.5
STEP_SIZE = 0.5
GAIN_RATE = 0.001
LINEAR_TERM = 3.4445
CUBIC_TERM = -4.775
QUINTIC_TERM = 2.0315
NORM_FLOOR = 1e-07
HIGHEST = lax.Precision.HIGHEST

@jax.custom_vjp
def low(v):
    return lax.optimization_barrier(v.astype(jnp.bfloat16)).astype(jnp.float32)

@jax.custom_vjp
def low_back(v):
    return v

def low_keep(v):
    return (low(v), None)

def low_pass(kept, grad):
    return (grad,)

def back_keep(v):
    return (v, None)

def back_low(kept, grad):
    return (low(grad),)
low.defvjp(low_keep, low_pass)
low_back.defvjp(back_keep, back_low)

def matmul(left, right):
    return jnp.dot(left, right, precision=HIGHEST)

def doc_positions(segment_row):
    length = segment_row.shape[0]
    places = jnp.arange(length, dtype=jnp.int32)
    starting = jnp.concatenate([jnp.ones((1,), dtype=bool), segment_row[1:] != segment_row[:-1]])
    first_index = lax.cummax(jnp.where(starting, places, jnp.zeros_like(places)), axis=0)
    return places - first_index

def rope_tables(positions):
    half_size = HD // 2
    frequency = ROPE_BASE ** (-2.0 * jnp.arange(half_size, dtype=jnp.float32) / HD)
    angles = positions.astype(jnp.float32)[:, None] * frequency[None, :]
    angles = jnp.concatenate([angles, angles], axis=-1)
    return (jnp.cos(angles)[:, None, :], jnp.sin(angles)[:, None, :])

def rotate(vectors, cosine_table, sine_table):
    half_size = vectors.shape[-1] // 2
    turned = jnp.concatenate([-vectors[..., half_size:], vectors[..., :half_size]], axis=-1)
    return vectors * cosine_table + turned * sine_table

def attend_block(query_block, query_segment, query_place, keys, values, key_segment, key_place):
    raw_scores = jnp.einsum('tgrd,kgd->grtk', query_block, keys, precision=HIGHEST)
    scores = low_back(raw_scores * HD ** (-0.5))
    allowed = (query_segment[:, None] == key_segment[None, :]) & (key_place[None, :] <= query_place[:, None])
    masked = jnp.where(allowed[None, None], scores, MASKED_SCORE)
    largest = lax.optimization_barrier(jnp.max(masked, axis=-1, keepdims=True))
    log_total = largest + jnp.log(lax.optimization_barrier(jnp.sum(jnp.exp(masked - largest), axis=-1, keepdims=True)))
    probabilities = low(jnp.exp(masked - log_total))
    return jnp.einsum('grtk,kgd->tgrd', probabilities, values, precision=HIGHEST)

def forward(params, gains, rows_in, segment_row):
    query_weight, key_weight, value_weight, output_weight, gate_weight, up_weight, down_weight = params
    length = rows_in.shape[0]
    group_size = H // KVH
    block_size = min(512, length)
    block_count = length // block_size
    cosine_table, sine_table = rope_tables(doc_positions(segment_row))
    inverse_first = lax.rsqrt(lax.optimization_barrier(jnp.mean(rows_in * rows_in, axis=-1, keepdims=True)) + EPSILON)
    act_first = low(rows_in * inverse_first * gains[0])
    query_pre = low_back(matmul(act_first, query_weight))
    key_pre = low_back(matmul(act_first, key_weight))
    value_pre = low(low_back(matmul(act_first, value_weight)))
    queries = low(rotate(query_pre.reshape(length, H, HD), cosine_table, sine_table))
    keys = low(rotate(key_pre.reshape(length, KVH, HD), cosine_table, sine_table))
    values = value_pre.reshape(length, KVH, HD)
    places = jnp.arange(length, dtype=jnp.int32)

    def one_block(inputs):
        query_block, query_segment, query_place = inputs
        return attend_block(query_block, query_segment, query_place, keys, values, segment_row, places)
    attended = lax.map(jax.checkpoint(one_block), (queries.reshape(block_count, block_size, KVH, group_size, HD), segment_row.reshape(block_count, block_size), places.reshape(block_count, block_size)))
    attended = low(low_back(attended.reshape(length, H * HD)))
    middle = rows_in + low_back(matmul(attended, output_weight))
    inverse_second = lax.rsqrt(lax.optimization_barrier(jnp.mean(middle * middle, axis=-1, keepdims=True)) + EPSILON)
    act_second = low(middle * inverse_second * gains[1])
    gate_pre = low_back(matmul(act_second, gate_weight))
    up_pre = low_back(matmul(act_second, up_weight))
    hidden = low(jax.nn.silu(gate_pre) * up_pre)
    return middle + low_back(matmul(hidden, down_weight))

def gram_of(iterate, leftward_flag):
    if leftward_flag:
        return jnp.dot(iterate, iterate.T, precision=HIGHEST)
    return jnp.dot(iterate.T, iterate, precision=HIGHEST)

def apply_gram(iterate, gram_matrix, leftward_flag):
    if leftward_flag:
        first_pass = jnp.dot(gram_matrix, iterate, precision=HIGHEST)
        second_pass = jnp.dot(gram_matrix, first_pass, precision=HIGHEST)
    else:
        first_pass = jnp.dot(iterate, gram_matrix, precision=HIGHEST)
        second_pass = jnp.dot(first_pass, gram_matrix, precision=HIGHEST)
    return LINEAR_TERM * iterate + CUBIC_TERM * first_pass + QUINTIC_TERM * second_pass

def orthogonal(moment, leftward_flag):
    iterate = moment / (jnp.sqrt(jnp.sum(moment * moment)) + NORM_FLOOR)
    for iteration in range(NS_STEPS):
        iterate = apply_gram(iterate, gram_of(iterate, leftward_flag), leftward_flag)
    return iterate

def reference(tokens, out_grad, segments, query_copy, key_copy, value_copy, output_copy, gate_copy, up_copy, down_copy, gains_copy, query_master, key_master, value_master, output_master, gate_master, up_master, down_master, gains_master, query_moment, key_moment, value_moment, output_moment, gate_moment, up_moment, down_moment, gains_moment):
    copies = (query_copy, key_copy, value_copy, output_copy, gate_copy, up_copy, down_copy)
    params = tuple((weight.astype(jnp.float32) for weight in copies))
    gains = gains_copy.astype(jnp.float32)

    def one_sequence(carried, inputs):
        rows_in, cotangent_row, segment_row = inputs
        result, pullback = jax.vjp(lambda weights, scales, source: forward(weights, scales, source, segment_row), params, gains, rows_in.astype(jnp.float32))
        weight_grads, gain_grads, input_grad = pullback(cotangent_row.astype(jnp.float32))
        summed = jax.tree.map(lambda running, addend: running + addend, carried, (weight_grads, gain_grads))
        return (summed, (result.astype(jnp.bfloat16), input_grad))
    initial = (tuple((jnp.zeros_like(weight) for weight in params)), jnp.zeros_like(gains))
    (weight_grads, gains_grad), (out_tokens, in_grad) = lax.scan(one_sequence, initial, (tokens, out_grad, segments))
    gradients = tuple(weight_grads) + (gains_grad,)
    moments = (query_moment, key_moment, value_moment, output_moment, gate_moment, up_moment, down_moment, gains_moment)
    masters = (query_master, key_master, value_master, output_master, gate_master, up_master, down_master)
    new_moments = tuple((MOMENTUM * previous + gradient for previous, gradient in zip(moments, gradients)))
    new_weights = []
    for master, moment in zip(masters, new_moments[:7]):
        rows_count, cols_count = master.shape
        factor = STEP_SIZE * math.sqrt(max(rows_count, cols_count) / rows_count)
        new_weights.append(master - factor * orthogonal(moment, rows_count < cols_count))
    new_weights.append(gains_master - GAIN_RATE * new_moments[7])
    rounded = tuple((weight.astype(jnp.bfloat16) for weight in new_weights))
    return (out_tokens, in_grad) + gradients + new_moments + tuple(new_weights) + rounded
```

```python
import functools
import math

import jax
import jax.numpy as jnp
from jax import lax
from jax.experimental import pallas as pl
from jax.experimental.pallas import tpu as pltpu
from jax.sharding import Mesh
from jax.sharding import PartitionSpec as P

H = 9
KVH = 3
HD = 64
GROUP = H // KVH
KVW = KVH * HD
NS_STEPS = 5

EPSILON = 1e-05
ROPE_BASE = 10000.0
MASKED_SCORE = -1e30
MOMENTUM = 0.5
STEP_SIZE = 0.5
GAIN_RATE = 0.001
LINEAR_TERM = 3.4445
CUBIC_TERM = -4.775
QUINTIC_TERM = 2.0315
NORM_FLOOR = 1e-07
SCALE = HD ** (-0.5)

F32 = jnp.float32
BF16 = jnp.bfloat16


NN = (((1,), (0,)), ((), ()))
NT = (((1,), (1,)), ((), ()))
TN = (((0,), (0,)), ((), ()))


def mm(left, right, dims=NN):
    return lax.dot_general(left, right, dims, preferred_element_type=F32)


def flip(value, axis, bit):
    size = lax.axis_size(axis)
    return lax.ppermute(value, axis, [(i, i ^ bit) for i in range(size)])


def bits_of(size):
    bits = []
    while size > 1:
        size //= 2
        bits.append(size)
    return bits


def gather_slots(value, stages):
    for axis, bit in stages:
        value = jnp.concatenate([value, flip(value, axis, bit)], axis=0)
    return value


def scatter_slots(sent, kept, stages):
    axis, bit = stages[-1]
    kept = kept + flip(sent, axis, bit).astype(F32)
    for axis, bit in reversed(stages[:-1]):
        half = kept.shape[0] // 2
        got = flip(kept[half:].astype(BF16), axis, bit)
        kept = kept[:half] + got.astype(F32)
    return kept


def whole_call(body, out_shape, scratch_shapes=()):
    return pl.pallas_call(
        body,
        out_shape=out_shape,
        scratch_shapes=scratch_shapes,
        compiler_params=pltpu.CompilerParams(vmem_limit_bytes=56 * 1024 * 1024),
    )


def turn_chunk(chunk, cosine, sine):
    lane = lax.broadcasted_iota(jnp.int32, chunk.shape, 1)
    turned = jnp.where(
        lane % HD < HD // 2,
        pltpu.roll(chunk, 128 - HD // 2, 1),
        pltpu.roll(chunk, HD // 2, 1),
    )
    return chunk * cosine + turned * sine


def turn_lanes(full, cosine, sine):
    width = full.shape[1]
    pieces = []
    for start in range(0, width - width % 128, 128):
        pieces.append(turn_chunk(full[:, start : start + 128], cosine, sine))
    if width % 128:
        last = full[:, width - 64 :]
        pieces.append(turn_chunk(jnp.concatenate([last, last], axis=1), cosine, sine)[:, :64])
    return jnp.concatenate(pieces, axis=1)


def kv_body(act_ref, weight_ref, cos_ref, sin_ref, out_ref):
    pre = mm(act_ref[...], weight_ref[...])
    turned = turn_lanes(pre, cos_ref[...], sin_ref[...])
    lane = lax.broadcasted_iota(jnp.int32, pre.shape, 1)
    out_ref[...] = jnp.where(lane < KVW, turned, pre).astype(BF16)


def query_body(act_ref, weight_ref, cos_ref, sin_ref, out_ref):
    pre = mm(act_ref[...], weight_ref[...])
    out_ref[...] = turn_lanes(pre, cos_ref[...], sin_ref[...]).astype(BF16)


def allowed_pairs(key_seg, query_seg, row_count):
    shape = (key_seg.shape[0], query_seg.shape[1])
    key_row = lax.broadcasted_iota(jnp.int32, shape, 0)
    query_col = lax.broadcasted_iota(jnp.int32, shape, 1)
    earlier = (key_row >= row_count) | (key_row <= query_col)
    return (key_seg == query_seg) & earlier


def attend_body(block_count, query_ref, *refs):
    kv_refs = refs[:block_count]
    key_seg_ref, query_seg_ref, out_ref, lse_ref = refs[block_count:]
    row_count = query_ref.shape[0]
    allowed = allowed_pairs(key_seg_ref[...], query_seg_ref[...], row_count)
    joined = jnp.concatenate([ref[...] for ref in kv_refs], axis=0)
    queries = query_ref[...]
    outs = []
    for head in range(H):
        group = head // GROUP
        keys = joined[:, group * HD : (group + 1) * HD]
        values = joined[:, KVW + group * HD : KVW + (group + 1) * HD]
        head_query = queries[:, head * HD : (head + 1) * HD]
        scores = jnp.where(allowed, mm(keys, head_query, NT) * SCALE, MASKED_SCORE)
        largest = jnp.max(scores, axis=0, keepdims=True)
        weights = jnp.exp(scores - largest)
        total = jnp.sum(weights, axis=0, keepdims=True)
        lse_ref[head : head + 1, :] = largest + jnp.log(total)
        probs = (weights * (1.0 / total)).astype(BF16)
        outs.append(mm(probs, values, TN))
    out_ref[...] = jnp.concatenate(outs, axis=1).astype(BF16)


def attend_back_body(block_count, query_ref, *refs):
    kv_refs = refs[:block_count]
    (key_seg_ref, query_seg_ref, rows_ref, lse_ref, cos_ref, sin_ref) = refs[
        block_count : block_count + 6
    ]
    query_out = refs[block_count + 6]
    block_outs = refs[block_count + 7 :]
    row_count = query_ref.shape[0]
    allowed = allowed_pairs(key_seg_ref[...], query_seg_ref[...], row_count)
    joined = jnp.concatenate([ref[...] for ref in kv_refs], axis=0)
    queries = query_ref[...]
    rows = rows_ref[...]
    query_parts, key_parts, value_parts = [], [], []
    for group in range(KVH):
        keys = joined[:, group * HD : (group + 1) * HD]
        values = joined[:, KVW + group * HD : KVW + (group + 1) * HD]
        key_sum, value_sum = None, None
        for head in range(group * GROUP, (group + 1) * GROUP):
            head_query = queries[:, head * HD : (head + 1) * HD]
            head_rows = rows[:, head * HD : (head + 1) * HD]
            scores = jnp.where(allowed, mm(keys, head_query, NT) * SCALE, MASKED_SCORE)
            exact = jnp.exp(scores - lse_ref[head : head + 1, :])
            dp = mm(values, head_rows, NT)
            weighted = exact * dp
            delta = jnp.sum(weighted, axis=0, keepdims=True)
            score_rows = (weighted - exact * delta).astype(BF16)
            query_parts.append(mm(score_rows, keys, TN) * SCALE)
            key_term = mm(score_rows, head_query)
            value_term = mm(exact.astype(BF16), head_rows)
            key_sum = key_term if key_sum is None else key_sum + key_term
            value_sum = value_term if value_sum is None else value_sum + value_term
        key_parts.append(key_sum * SCALE)
        value_parts.append(value_sum)
    query_sum = jnp.concatenate(query_parts, axis=1)
    query_out[...] = turn_lanes(query_sum, cos_ref[...], -sin_ref[...]).astype(BF16)
    joined_sum = jnp.concatenate(key_parts + value_parts, axis=1)
    for index, ref in enumerate(block_outs):
        ref[...] = joined_sum[index * row_count : (index + 1) * row_count].astype(ref.dtype)


def kv_rows_body(block_count, *refs):
    parts, cos_ref, sin_ref, out_ref = refs[:block_count], refs[-3], refs[-2], refs[-1]
    total = parts[0][...]
    for part in parts[1:]:
        total = total + part[...].astype(F32)
    turned = turn_lanes(total, cos_ref[...], -sin_ref[...])
    lane = lax.broadcasted_iota(jnp.int32, total.shape, 1)
    out_ref[...] = jnp.where(lane < KVW, turned, total).astype(BF16)


def polar_steps(wide_ref):
    size = wide_ref.shape[0]
    first = wide_ref[...]
    norm = jnp.sqrt(jnp.sum(first * first)) + NORM_FLOOR
    wide_ref[...] = first / norm

    def step(index, carry):
        row = lax.broadcasted_iota(jnp.int32, (size, size), 0)
        col = lax.broadcasted_iota(jnp.int32, (size, size), 1)
        diagonal = row == col
        rounded = wide_ref[...].astype(BF16)
        gram = mm(rounded, rounded, NT)
        mean = jnp.sum(jnp.where(diagonal, gram, 0.0)) / size
        rest = gram - jnp.where(diagonal, mean, 0.0)
        rest_rounded = rest.astype(BF16)
        square = mm(rest_rounded, rest_rounded) + (2.0 * mean) * rest
        square = square + jnp.where(diagonal, mean * mean, 0.0)
        poly = CUBIC_TERM * gram + QUINTIC_TERM * square
        shift = jnp.sum(jnp.where(diagonal, poly, 0.0)) / size
        poly_rest = (poly - jnp.where(diagonal, shift, 0.0)).astype(BF16)
        wide_ref[...] = (LINEAR_TERM + shift) * wide_ref[...] + mm(poly_rest, rounded)
        return carry

    lax.fori_loop(0, NS_STEPS, step, 0)


def big_body(shard_rows, returned, in_ref, out_ref, wide_ref):
    slots = in_ref.shape[0]
    tall = jnp.concatenate([in_ref[s, :shard_rows, :] for s in range(slots)], axis=0)
    wide_ref[...] = jnp.transpose(tall.astype(F32))
    polar_steps(wide_ref)
    result = jnp.transpose(wide_ref[:, : returned * shard_rows]).astype(BF16)
    out_ref[...] = jnp.zeros(out_ref.shape, BF16)
    for s in range(returned):
        out_ref[s, :shard_rows, :] = result[s * shard_rows : (s + 1) * shard_rows]


def small_body(pad_rows, returned, in_ref, out_ref, query_ref, output_ref, key_ref, value_ref):
    slots = in_ref.shape[0]
    out_ref[...] = jnp.zeros(out_ref.shape, BF16)
    places = (
        (query_ref, 0, 0),
        (output_ref, pad_rows, 0),
        (key_ref, 2 * pad_rows, 0),
        (value_ref, 2 * pad_rows, KVW),
    )
    for ref, first, lane in places:
        width = ref.shape[0]
        tall = jnp.concatenate(
            [in_ref[s, first : first + pad_rows, lane : lane + width] for s in range(slots)],
            axis=0,
        )
        ref[...] = jnp.transpose(tall.astype(F32))
        polar_steps(ref)
    for ref, first in ((query_ref, 0), (output_ref, pad_rows)):
        result = jnp.transpose(ref[:, : returned * pad_rows]).astype(BF16)
        for s in range(returned):
            out_ref[s, first : first + pad_rows, :] = result[s * pad_rows : (s + 1) * pad_rows]
    result = jnp.transpose(
        jnp.concatenate(
            [key_ref[:, : returned * pad_rows], value_ref[:, : returned * pad_rows]], axis=0
        )
    ).astype(BF16)
    for s in range(returned):
        out_ref[s, 2 * pad_rows : 3 * pad_rows, : 2 * KVW] = result[
            s * pad_rows : (s + 1) * pad_rows
        ]


def local(
    tokens,
    out_grad,
    segments,
    query_copy,
    key_copy,
    value_copy,
    output_copy,
    gate_copy,
    up_copy,
    down_copy,
    gains_copy,
    query_master,
    key_master,
    value_master,
    output_master,
    gate_master,
    up_master,
    down_master,
    gains_master,
    query_moment,
    key_moment,
    value_moment,
    output_moment,
    gate_moment,
    up_moment,
    down_moment,
    gains_moment,
):
    x_size, z_size = lax.axis_size("x"), lax.axis_size("ctx")
    x_at, core_at, z_at = lax.axis_index("x"), lax.axis_index("core"), lax.axis_index("ctx")
    z_bits, x_bits = bits_of(z_size), bits_of(x_size)
    mlp_stages = [("ctx", b) for b in z_bits] + [("x", b) for b in x_bits]
    all_stages = mlp_stages + [("core", 1)]
    slots = 2 * x_size * z_size
    rows, width = tokens.shape[1], tokens.shape[2]
    length = segments.shape[1]
    shard = query_copy.shape[0]
    pad = -(-(shard + 2) // 8) * 8
    hidden_shard = down_copy.shape[0]
    back_blocks = z_size // 2

    kv_shard = jnp.concatenate([key_copy, value_copy], axis=1)
    gain_rows = jnp.pad(gains_copy, ((0, pad - shard - 2), (0, 2 * KVW - shard)))
    kv_slots = gather_slots(jnp.concatenate([kv_shard, gain_rows], axis=0), all_stages)
    pad_shard = ((0, pad - shard), (0, 0))
    qo_slots = gather_slots(
        jnp.concatenate([jnp.pad(query_copy, pad_shard), jnp.pad(output_copy, pad_shard)], axis=0),
        all_stages,
    )
    gate_slots = gather_slots(gate_copy.T, mlp_stages)
    up_slots = gather_slots(up_copy.T, mlp_stages)
    down_slots = gather_slots(down_copy, mlp_stages)
    other_grad = flip(out_grad[0], "core", 1)

    def device_of(position):
        z_part, x_part, core_part = z_at, x_at, core_at
        for index, (axis, bit) in enumerate(all_stages):
            part = ((position >> index) & 1) * bit
            if axis == "ctx":
                z_part = z_part ^ part
            elif axis == "x":
                x_part = x_part ^ part
            else:
                core_part = core_part ^ part
        return (x_part * 2 + core_part) * z_size + z_part

    def placing(slot_rows, first):
        column = lax.broadcasted_iota(jnp.int32, (1, slots * slot_rows), 1)
        inside = column % slot_rows - first
        feature = device_of(column // slot_rows) * shard + inside
        feature = jnp.where((inside >= 0) & (inside < shard), feature, -1)
        return (lax.broadcasted_iota(jnp.int32, (width, 1), 0) == feature).astype(BF16)

    place_kv = placing(pad, 0)
    place_query = placing(2 * pad, 0)
    place_output = placing(2 * pad, pad)

    segment_row = segments[0]
    row_start = z_at * rows
    query_segment = lax.dynamic_slice_in_dim(segment_row, row_start, rows)
    first_index = jnp.sum(
        (segment_row[None, :] < query_segment[:, None]).astype(jnp.int32), axis=1, keepdims=True
    )
    positions = (row_start + jnp.arange(rows, dtype=jnp.int32)[:, None] - first_index).astype(F32)
    lane = jnp.arange(128, dtype=jnp.int32)
    frequency = ROPE_BASE ** (-2.0 * (lane % (HD // 2)).astype(F32) / HD)
    angles = positions * frequency[None, :]
    sign = jnp.where(lane % HD < HD // 2, -1.0, 1.0).astype(F32)
    cosine, sine = jnp.cos(angles), jnp.sin(angles) * sign[None, :]
    key_segments = [query_segment]
    for back in range(1, back_blocks + 1):
        at = jnp.maximum(row_start - back * rows, 0)
        piece = lax.dynamic_slice_in_dim(segment_row, at, rows)
        key_segments.append(jnp.where(z_at >= back, piece, -1))
    key_seg = jnp.concatenate(key_segments)[:, None]
    query_seg = query_segment[None, :]

    rows_in = tokens[0].astype(F32)
    inverse_first = lax.rsqrt(jnp.mean(rows_in * rows_in, axis=-1, keepdims=True) + EPSILON)
    normed_first = rows_in * inverse_first
    gain_slots = kv_slots.reshape(slots, pad, 2 * KVW)[:, shard : shard + 2, :shard]
    spread = (
        lax.broadcasted_iota(jnp.int32, (shard, width), 1) % shard
        == lax.broadcasted_iota(jnp.int32, (shard, width), 0)
    ).astype(BF16)
    owner = device_of(lax.broadcasted_iota(jnp.int32, (slots, 1), 0))
    mine = owner == lax.broadcasted_iota(jnp.int32, (slots, width), 1) // shard
    gains = [
        jnp.sum(jnp.where(mine, mm(gain_slots[:, i], spread), 0.0), axis=0, keepdims=True)
        for i in range(2)
    ]
    act_first = (normed_first * gains[0]).astype(BF16)
    act_kv = mm(act_first, place_kv).astype(BF16)
    kv_own = whole_call(kv_body, jax.ShapeDtypeStruct((rows, 2 * KVW), BF16))(
        act_kv, kv_slots, cosine, sine
    )
    kv_blocks = [kv_own]
    for back in range(1, back_blocks + 1):
        pairs = [(i, i + back) for i in range(z_size - back)]
        kv_blocks.append(lax.ppermute(kv_own, "ctx", pairs))
    act_query = mm(act_first, place_query).astype(BF16)
    queries = whole_call(query_body, jax.ShapeDtypeStruct((rows, width), BF16))(
        act_query, qo_slots, cosine, sine
    )

    block_count = back_blocks + 1
    attended, lse = whole_call(
        functools.partial(attend_body, block_count),
        (
            jax.ShapeDtypeStruct((rows, width), BF16),
            jax.ShapeDtypeStruct((H, rows), F32),
        ),
    )(queries, *kv_blocks, key_seg, query_seg)
    act_output = mm(attended, place_output).astype(BF16)
    middle = rows_in + mm(act_output, qo_slots)

    inverse_second = lax.rsqrt(jnp.mean(middle * middle, axis=-1, keepdims=True) + EPSILON)
    normed_second = middle * inverse_second
    act_second = (normed_second * gains[1]).astype(BF16)
    acts = jnp.concatenate([act_second, flip(act_second, "core", 1)], axis=0)
    mlp_rows = jnp.concatenate([out_grad[0], other_grad], axis=0)
    gate_pre = mm(acts, gate_slots, NT)
    up_pre = mm(acts, up_slots, NT)
    gate_sigmoid = jax.nn.sigmoid(gate_pre)
    gate_silu = gate_pre * gate_sigmoid
    hidden = (gate_silu * up_pre).astype(BF16)
    half = hidden.shape[1] // 2
    down_sent = mm(hidden[:, half:], mlp_rows, TN).astype(BF16)
    hidden_rows = mm(mlp_rows, down_slots, NT)
    gate_rows = (
        hidden_rows * up_pre * gate_sigmoid * (1.0 + gate_pre * (1.0 - gate_sigmoid))
    ).astype(BF16)
    up_rows = (hidden_rows * gate_silu).astype(BF16)
    second_part = mm(gate_rows, gate_slots) + mm(up_rows, up_slots)
    second_back = second_part[:rows] + flip(second_part[rows:].astype(BF16), "core", 1).astype(F32)
    gate_sent = mm(gate_rows[:, half:], acts, TN).astype(BF16)
    up_sent = mm(up_rows[:, half:], acts, TN).astype(BF16)
    down_total = scatter_slots(down_sent, mm(hidden[:, :half], mlp_rows, TN), mlp_stages)
    gate_total = scatter_slots(gate_sent, mm(gate_rows[:, :half], acts, TN), mlp_stages)
    up_total = scatter_slots(up_sent, mm(up_rows[:, :half], acts, TN), mlp_stages)
    result_part = mm(hidden, down_slots)
    result = (
        middle
        + result_part[:rows]
        + flip(result_part[rows:].astype(BF16), "core", 1).astype(F32)
    )

    result_grad = out_grad[0].astype(F32)
    second_gain = jnp.sum(second_back * normed_second, axis=0, keepdims=True)
    scaled = second_back * gains[1]
    middle_grad = result_grad + inverse_second * (
        scaled - normed_second * jnp.mean(scaled * normed_second, axis=-1, keepdims=True)
    )
    attn_rows = middle_grad.astype(BF16)
    back_slots = mm(attn_rows, qo_slots, NT).astype(BF16)
    attended_rows = mm(back_slots, place_output, NT).astype(BF16)
    outs = whole_call(
        functools.partial(attend_back_body, block_count),
        (
            jax.ShapeDtypeStruct((rows, width), BF16),
            jax.ShapeDtypeStruct((rows, 2 * KVW), F32),
        )
        + (jax.ShapeDtypeStruct((rows, 2 * KVW), BF16),) * back_blocks,
    )(queries, *kv_blocks, key_seg, query_seg, attended_rows, lse, cosine, sine)
    query_rows = outs[0]
    kv_terms = [outs[1]]
    for back in range(1, back_blocks + 1):
        pairs = [(i + back, i) for i in range(z_size - back)]
        kv_terms.append(lax.ppermute(outs[1 + back], "ctx", pairs))
    kv_rows = whole_call(
        functools.partial(kv_rows_body, block_count),
        jax.ShapeDtypeStruct((rows, 2 * KVW), BF16),
    )(*kv_terms, cosine, sine)

    both_acts = jnp.concatenate([act_query, act_output], axis=0)
    both_rows = jnp.concatenate([query_rows, attn_rows], axis=0)
    qo_half = slots * pad
    qo_sent = mm(both_acts[:, qo_half:], both_rows, TN).astype(BF16)
    qo_total = scatter_slots(qo_sent, mm(both_acts[:, :qo_half], both_rows, TN), all_stages)
    query_back = mm(query_rows, qo_slots, NT)
    kv_back = mm(kv_rows, kv_slots, NT)

    def canonical(value, place):
        high = value.astype(BF16)
        low = (value - high.astype(F32)).astype(BF16)
        return mm(high, place, NT) + mm(low, place, NT)

    first_back = canonical(query_back, place_query) + canonical(kv_back, place_kv)
    first_gain = jnp.sum(first_back * normed_first, axis=0, keepdims=True)
    scaled = first_back * gains[0]
    input_grad = middle_grad + inverse_first * (
        scaled - normed_first * jnp.mean(scaled * normed_first, axis=-1, keepdims=True)
    )
    gain_parts = [
        lax.dot_general(
            jnp.where(mine, gain, 0.0),
            spread.astype(F32),
            NT,
            precision=lax.Precision.HIGHEST,
            preferred_element_type=F32,
        )
        for gain in (first_gain, second_gain)
    ]
    gain_block = jnp.pad(
        jnp.stack(gain_parts, axis=1), ((0, 0), (shard, pad - shard - 2), (0, 2 * KVW - shard))
    )
    kv_local = mm(act_kv, kv_rows, TN) + gain_block.reshape(slots * pad, 2 * KVW)
    kv_half = slots * pad // 2
    kv_total = scatter_slots(kv_local[kv_half:].astype(BF16), kv_local[:kv_half], all_stages)

    def copies_sum(value):
        own = value.astype(BF16)
        return own.astype(F32) + flip(own, "rep", 1).astype(F32)

    mlp_total = copies_sum(jnp.concatenate([gate_total, up_total, down_total], axis=0))
    gate_grad_t = mlp_total[:hidden_shard]
    up_grad_t = mlp_total[hidden_shard : 2 * hidden_shard]
    down_grad = mlp_total[2 * hidden_shard :]
    qo_total = copies_sum(qo_total)
    kv_total = copies_sum(kv_total)
    totals = (
        qo_total[:shard],
        kv_total[:shard, :KVW],
        kv_total[:shard, KVW:],
        qo_total[pad : pad + shard],
        gate_grad_t.T,
        up_grad_t.T,
        down_grad,
        kv_total[shard : shard + 2, :shard],
    )
    moments = (
        query_moment,
        key_moment,
        value_moment,
        output_moment,
        gate_moment,
        up_moment,
        down_moment,
        gains_moment,
    )
    new_moments = tuple(MOMENTUM * m + g for m, g in zip(moments, totals))

    message_rows = max(hidden_shard, 3 * pad)
    if z_size % 4:
        raise ValueError("ctx size")
    stride = z_size // 4

    def as_message(value):
        value = value.astype(BF16)
        return jnp.pad(value, ((0, message_rows - value.shape[0]), (0, 0)))

    moment_pad = ((0, pad - shard), (0, 0))
    kv_moment = jnp.concatenate([new_moments[1], new_moments[2]], axis=1)
    messages = jnp.stack(
        [
            as_message(MOMENTUM * gate_moment.T + gate_grad_t),
            as_message(MOMENTUM * up_moment.T + up_grad_t),
            as_message(new_moments[6]),
            as_message(
                jnp.concatenate(
                    [
                        jnp.pad(new_moments[0], moment_pad),
                        jnp.pad(new_moments[3], moment_pad),
                        jnp.pad(kv_moment, ((0, pad - shard), (0, width - 2 * KVW))),
                    ],
                    axis=0,
                )
            ),
        ]
    )

    def picked(stack, index):
        return lax.dynamic_index_in_dim(stack, index, 0, keepdims=False)

    owner_columns = [g * stride for g in range(4)]
    arrived = [picked(messages, z_at // stride)]
    for other in range(1, z_size):
        pairs = [(d ^ other, d) for d in owner_columns]
        arrived.append(lax.ppermute(picked(messages, (z_at ^ other) // stride), "ctx", pairs))
    stack = jnp.stack(arrived)
    stack = gather_slots(stack, [("x", b) for b in x_bits] + [("core", 1)])

    out_type = jax.ShapeDtypeStruct((z_size, message_rows, width), BF16)
    big = whole_call(
        functools.partial(big_body, hidden_shard, z_size),
        out_type,
        [pltpu.VMEM((width, slots * hidden_shard), F32)],
    )
    small = whole_call(
        functools.partial(small_body, pad, z_size),
        out_type,
        [
            pltpu.VMEM((width, slots * pad), F32),
            pltpu.VMEM((width, slots * pad), F32),
            pltpu.VMEM((KVW, slots * pad), F32),
            pltpu.VMEM((KVW, slots * pad), F32),
        ],
    )
    solved = lax.cond(z_at // stride == 3, small, big, stack)
    returned = [solved[0]]
    for other in range(1, z_size):
        pairs = [(d, d ^ other) for d in owner_columns]
        returned.append(lax.ppermute(solved[other], "ctx", pairs))
    returned = jnp.stack(returned)
    by_group = [picked(returned, z_at ^ column) for column in owner_columns]
    gate_polar = by_group[0][:hidden_shard].T.astype(F32)
    up_polar = by_group[1][:hidden_shard].T.astype(F32)
    down_polar = by_group[2][:hidden_shard].astype(F32)
    rest = by_group[3]
    polars = (
        rest[:shard].astype(F32),
        rest[2 * pad : 2 * pad + shard, :KVW].astype(F32),
        rest[2 * pad : 2 * pad + shard, KVW : 2 * KVW].astype(F32),
        rest[pad : pad + shard].astype(F32),
        gate_polar,
        up_polar,
        down_polar,
    )
    masters = (
        query_master,
        key_master,
        value_master,
        output_master,
        gate_master,
        up_master,
        down_master,
    )
    inner = slots * hidden_shard
    full_shapes = (
        (width, width),
        (width, KVW),
        (width, KVW),
        (width, width),
        (width, inner),
        (width, inner),
        (inner, width),
    )
    new_weights = []
    for master, polar, shape in zip(masters, polars, full_shapes):
        factor = STEP_SIZE * math.sqrt(max(shape) / shape[0])
        new_weights.append(master - factor * polar)
    new_weights.append(gains_master - GAIN_RATE * new_moments[7])
    rounded = tuple(weight.astype(BF16) for weight in new_weights)
    return (
        (result[None].astype(BF16), input_grad[None])
        + tuple(totals)
        + new_moments
        + tuple(new_weights)
        + rounded
    )


def solution(mesh):
    dp_size, ctx_size, rep_size = (mesh.shape[name] for name in ("dp", "ctx", "rep"))
    split = Mesh(
        mesh.devices.reshape(dp_size // 2, 2, ctx_size, rep_size), ("x", "core", "ctx", "rep")
    )
    batch = ("x", "core", "rep")
    parts = ("x", "core", "ctx")
    by_row, by_column = P(parts, None), P(None, parts)
    weights = (by_row, by_row, by_row, by_row, by_column, by_column, by_row, by_column)
    token_spec = P(batch, "ctx", None)
    return jax.shard_map(
        local,
        mesh=split,
        in_specs=(token_spec, token_spec, P(batch, None)) + weights * 3,
        out_specs=(token_spec, token_spec) + weights * 4,
        check_vma=False,
    )
```

```python
import functools
import math

import jax
import jax.numpy as jnp
import numpy as np
from jax import lax
from jax.experimental import pallas as pl
from jax.experimental.pallas import tpu as pltpu
from jax.sharding import Mesh
from jax.sharding import PartitionSpec as P

H = 9
KVH = 3
HD = 64
GROUP = H // KVH
KVW = KVH * HD
NS_STEPS = 5

EPSILON = 1e-05
ROPE_BASE = 10000.0
MASKED_SCORE = -1e30
MOMENTUM = 0.5
STEP_SIZE = 0.5
GAIN_RATE = 0.001
LINEAR_TERM = 3.4445
CUBIC_TERM = -4.775
QUINTIC_TERM = 2.0315
NORM_FLOOR = 1e-07
SCALE = HD ** (-0.5)

F32 = jnp.float32
BF16 = jnp.bfloat16


NN = (((1,), (0,)), ((), ()))
NT = (((1,), (1,)), ((), ()))
TN = (((0,), (0,)), ((), ()))


def mm(left, right, dims=NN):
    return lax.dot_general(left, right, dims, preferred_element_type=F32)


def flip(value, axis, bit):
    size = lax.axis_size(axis)
    return lax.ppermute(value, axis, [(i, i ^ bit) for i in range(size)])


def bits_of(size):
    bits = []
    while size > 1:
        size //= 2
        bits.append(size)
    return bits


def call(body, out_shape, *operands, scratch=(), scalars=0, after=()):
    count = len(operands)
    specs = [pl.BlockSpec(memory_space=pltpu.SMEM)] * scalars
    specs += [pl.BlockSpec(memory_space=pltpu.VMEM)] * (count - scalars)
    specs += [pl.BlockSpec(memory_space=pl.ANY)] * len(after)

    def used(*refs):
        body(*refs[:count], *refs[count + len(after) :])

    return pl.pallas_call(
        used,
        out_shape=out_shape,
        in_specs=specs,
        scratch_shapes=scratch,
        compiler_params=pltpu.CompilerParams(vmem_limit_bytes=56 * 1024 * 1024),
    )(*operands, *after)


def shaped(dtype, *shape):
    return jax.ShapeDtypeStruct(shape, dtype)


def turn_chunk(chunk, cosine, sine):
    lane = lax.broadcasted_iota(jnp.int32, chunk.shape, 1)
    turned = jnp.where(
        lane % HD < HD // 2,
        pltpu.roll(chunk, 128 - HD // 2, 1),
        pltpu.roll(chunk, HD // 2, 1),
    )
    return chunk * cosine + turned * sine


def turn_lanes(full, cosine, sine):
    width = full.shape[1]
    pieces = []
    for start in range(0, width - width % 128, 128):
        pieces.append(turn_chunk(full[:, start : start + 128], cosine, sine))
    if width % 128:
        last = full[:, width - 64 :]
        pieces.append(turn_chunk(jnp.concatenate([last, last], axis=1), cosine, sine)[:, :64])
    return jnp.concatenate(pieces, axis=1)


def allowed_pairs(key_seg, query_seg, row_count):
    shape = (key_seg.shape[0], query_seg.shape[1])
    key_row = lax.broadcasted_iota(jnp.int32, shape, 0)
    query_col = lax.broadcasted_iota(jnp.int32, shape, 1)
    earlier = (key_row >= row_count) | (key_row <= query_col)
    return (key_seg == query_seg) & earlier


def placed(feature, width):
    at = lax.broadcasted_iota(jnp.int32, (width, feature.shape[1]), 0)
    return jnp.where(at == feature, 1.0, 0.0).astype(BF16)


def stacked(refs):
    return jnp.concatenate([ref[...] for ref in refs], axis=0)


def inverse_norm(value):
    return lax.rsqrt(jnp.mean(value * value, axis=-1, keepdims=True) + EPSILON)


FULL = 4


def cut(rows):
    return min(rows, -(-((rows + 1) // 2) // 16) * 16)


def packed_rows(rows):
    return FULL * rows + cut(rows)


def store_packed(out, base, value):
    rows, dtype = value.shape[0], out.dtype
    low = cut(rows)
    for index in range(FULL):
        at = base + index * rows
        out[at : at + rows, :] = value[:, index * 128 : (index + 1) * 128].astype(dtype)
    at = base + FULL * rows
    out[at : at + low, 0:64] = value[:low, FULL * 128 :].astype(dtype)
    if rows - low < low:
        out[at : at + low, 64:128] = jnp.zeros((low, 64), dtype)
    if rows > low:
        out[at : at + rows - low, 64:128] = value[low:, FULL * 128 :].astype(dtype)


def load_packed(refs, slot_rows, base, rows):
    places = [(ref, at + base) for ref in refs for at in range(0, ref.shape[0], slot_rows)]
    low = cut(rows)
    columns = []
    for index in range(FULL):
        columns.append(
            jnp.concatenate(
                [ref[at + index * rows : at + (index + 1) * rows, :] for ref, at in places], axis=0
            )
        )
    rest = []
    for ref, at in places:
        first = at + FULL * rows
        rest.append(ref[first : first + low, 0:64])
        if rows > low:
            rest.append(ref[first : first + rows - low, 64:128])
    columns.append(jnp.concatenate(rest, axis=0))
    return jnp.concatenate(columns, axis=1)


def store_pair(out, base, pad, first, second):
    for which, value in enumerate((first, second)):
        for index in range(FULL):
            at = base + (which * FULL + index) * pad
            out[at : at + pad, :] = value[:, index * 128 : (index + 1) * 128].astype(out.dtype)
        at = base + 2 * FULL * pad
        out[at : at + pad, which * 64 : which * 64 + 64] = value[:, FULL * 128 :].astype(out.dtype)


def load_pair(refs, slot_rows, pad, which):
    places = [(ref, at) for ref in refs for at in range(0, ref.shape[0], slot_rows)]
    columns = []
    for index in range(FULL):
        first = (which * FULL + index) * pad
        columns.append(
            jnp.concatenate([ref[at + first : at + first + pad, :] for ref, at in places], axis=0)
        )
    first = 2 * FULL * pad
    columns.append(
        jnp.concatenate(
            [
                ref[at + first : at + first + pad, which * 64 : which * 64 + 64]
                for ref, at in places
            ],
            axis=0,
        )
    )
    return jnp.concatenate(columns, axis=1)


def store_three(out, base, pad, value):
    for index in range(3):
        at = base + index * pad
        out[at : at + pad, :] = value[:, index * 128 : (index + 1) * 128].astype(out.dtype)


def load_three(refs, slot_rows, base, pad):
    places = [(ref, at + base) for ref in refs for at in range(0, ref.shape[0], slot_rows)]
    columns = [
        jnp.concatenate(
            [ref[at + index * pad : at + (index + 1) * pad, :] for ref, at in places], axis=0
        )
        for index in range(3)
    ]
    return jnp.concatenate(columns, axis=1)


def kv_message_body(shard, key_ref, value_ref, gains_ref, out_ref):
    out_ref[...] = jnp.zeros(out_ref.shape, BF16)
    out_ref[0:shard, 0:KVW] = key_ref[...]
    out_ref[0:shard, KVW : 2 * KVW] = value_ref[...]
    out_ref[shard : shard + 2, 0:shard] = gains_ref[...]


def qo_message_body(shard, pad, query_ref, output_ref, out_ref):
    out_ref[...] = jnp.zeros(out_ref.shape, BF16)
    for which, ref in enumerate((query_ref, output_ref)):
        for index in range(FULL):
            at = (which * FULL + index) * pad
            out_ref[at : at + shard, :] = ref[:, index * 128 : (index + 1) * 128]
        at = 2 * FULL * pad
        out_ref[at : at + shard, which * 64 : which * 64 + 64] = ref[:, FULL * 128 :]


def feed_message_body(at_ref, gate_ref, up_ref, out_ref):
    chosen = jnp.where(at_ref[2] == 0, gate_ref[...].astype(F32), up_ref[...].astype(F32))
    store_packed(out_ref, 0, chosen)


def down_message_body(down_ref, out_ref):
    store_packed(out_ref, 0, down_ref[...])


def setup_body(blocks, at_ref, tok_ref, grad_ref, seg_ref, frequency_ref, tok_out, grad_out,
               cos_out, sin_out, key_seg_out, query_seg_out):
    rows = tok_ref.shape[1]
    tok_out[...] = jnp.transpose(tok_ref[...])
    grad_out[...] = jnp.transpose(grad_ref[...])
    z_at = at_ref[0]

    def upright(row):
        return jnp.transpose(jnp.broadcast_to(row, (8, rows)))[:, 0:1]

    own = seg_ref[pl.ds(z_at, 1), :].astype(F32)
    own_column = upright(own)
    query_seg_out[...] = own
    key_seg_out[0:rows, :] = own_column
    for back in range(1, blocks):
        row = seg_ref[pl.ds(jnp.maximum(z_at - back, 0), 1), :].astype(F32)
        row = jnp.where(z_at >= back, row, -1.0)
        key_seg_out[back * rows : (back + 1) * rows, :] = upright(row)
    first = jnp.zeros((rows, 1), F32)
    for block in range(seg_ref.shape[0]):
        smaller = seg_ref[block : block + 1, :].astype(F32) < own_column
        first = first + jnp.sum(jnp.where(smaller, 1.0, 0.0), axis=1, keepdims=True)
    index = lax.broadcasted_iota(jnp.int32, (rows, 1), 0) + z_at * rows
    angles = (index.astype(F32) - first) * frequency_ref[...]
    lane = lax.broadcasted_iota(jnp.int32, angles.shape, 1)
    cos_out[...] = jnp.cos(angles)
    sin_out[...] = jnp.sin(angles) * jnp.where(lane % HD < HD // 2, -1.0, 1.0)


def join_body(*refs):
    out = refs[-1]
    at = 0
    for ref in refs[:-1]:
        out[at : at + ref.shape[0], :] = ref[...]
        at += ref.shape[0]


def kv_body(shard, pad, pieces, tok_ref, feature_ref, owner_ref, cos_ref, sin_ref, *refs):
    kv_out, act_out, act_kv_out, gains_out = refs[pieces:]
    weights = stacked(refs[:pieces])
    source = tok_ref[...].astype(F32)
    width = source.shape[1]
    slots = owner_ref.shape[0]
    place_at = lax.broadcasted_iota(jnp.int32, (slots, slots * pad), 1)
    slot_at = lax.broadcasted_iota(jnp.int32, (slots, slots * pad), 0)
    spread = spread_lanes(shard, 2 * KVW, width)
    mine = owner_ref[...] == lax.broadcasted_iota(jnp.int32, (slots, width), 1) // shard
    gains_out[...] = jnp.zeros(gains_out.shape, F32)
    for index in range(2):
        pick = jnp.where(place_at == slot_at * pad + shard + index, 1.0, 0.0).astype(BF16)
        by_slot = mm(pick, weights).astype(BF16)
        gain = jnp.sum(jnp.where(mine, mm(by_slot, spread), 0.0), axis=0, keepdims=True)
        gains_out[index : index + 1, :] = gain
    act = (source * inverse_norm(source) * gains_out[0:1, :]).astype(BF16)
    act_out[...] = act
    act_kv = mm(act, placed(feature_ref[...], width)).astype(BF16)
    act_kv_out[...] = act_kv
    pre = mm(act_kv, weights)
    turned = turn_lanes(pre, cos_ref[...], sin_ref[...])
    lane = lax.broadcasted_iota(jnp.int32, pre.shape, 1)
    kv_out[...] = jnp.where(lane < KVW, turned, pre).astype(BF16)


def spread_lanes(shard, lanes, width):
    lane = lax.broadcasted_iota(jnp.int32, (lanes, width), 0)
    feature = lax.broadcasted_iota(jnp.int32, (lanes, width), 1)
    return jnp.where((feature % shard == lane) & (lane < shard), 1.0, 0.0).astype(BF16)


def query_body(pad, act_ref, cos_ref, sin_ref, *refs):
    weights = load_pair(refs[:-1], 9 * pad, pad, 0)
    pre = mm(act_ref[...], weights)
    refs[-1][...] = turn_lanes(pre, cos_ref[...], sin_ref[...]).astype(BF16)


def attend_body(pad, pieces, blocks, query_ref, key_seg_ref, query_seg_ref, feature_ref, tok_ref,
                gains_ref, *refs):
    lse_ref, act_out, middle_out, second_out = refs[pieces + blocks :]
    row_count = query_ref.shape[0]
    allowed = allowed_pairs(key_seg_ref[...], query_seg_ref[...], row_count)
    joined = stacked(refs[pieces : pieces + blocks])
    queries = query_ref[...]
    outs = []
    for head in range(H):
        group = head // GROUP
        keys = joined[:, group * HD : (group + 1) * HD]
        values = joined[:, KVW + group * HD : KVW + (group + 1) * HD]
        head_query = queries[:, head * HD : (head + 1) * HD]
        scores = jnp.where(allowed, mm(keys, head_query, NT) * SCALE, MASKED_SCORE)
        largest = jnp.max(scores, axis=0, keepdims=True)
        weights = jnp.exp(scores - largest)
        total = jnp.sum(weights, axis=0, keepdims=True)
        lse_ref[head : head + 1, :] = largest + jnp.log(total)
        probs = (weights * (1.0 / total)).astype(BF16)
        outs.append(mm(probs, values, TN))
    attended = jnp.concatenate(outs, axis=1).astype(BF16)
    act = mm(attended, placed(feature_ref[...], attended.shape[1])).astype(BF16)
    act_out[...] = act
    middle = tok_ref[...].astype(F32) + mm(act, load_pair(refs[:pieces], 9 * pad, pad, 1))
    middle_out[...] = middle
    second_out[...] = (middle * inverse_norm(middle) * gains_ref[1:2, :]).astype(BF16)


def feed_body(hidden, pieces, at_ref, act_ref, other_ref, grad_ref, other_grad_ref, *refs):
    slot_rows = packed_rows(hidden)
    mine = load_packed(refs[:pieces], slot_rows, 0, hidden)
    copied = load_packed(refs[pieces : 2 * pieces], slot_rows, 0, hidden)
    down_weight = load_packed(refs[2 * pieces : 3 * pieces], slot_rows, 0, hidden)
    hidden_out, gate_out, up_out, own_out, send_out = refs[3 * pieces :]
    row_count = act_ref.shape[0]
    acts = jnp.concatenate([act_ref[...], other_ref[...]], axis=0)
    grads = jnp.concatenate([grad_ref[...], other_grad_ref[...]], axis=0)
    first = at_ref[2] == 0
    gate_weight = jnp.where(first, mine, copied)
    up_weight = jnp.where(first, copied, mine)
    gate = mm(acts, gate_weight, NT)
    up = mm(acts, up_weight, NT)
    back = mm(grads, down_weight, NT)
    sigmoid = jax.nn.sigmoid(gate)
    silu = gate * sigmoid
    hidden_out[...] = (silu * up).astype(BF16)
    gate_rows = (back * up * sigmoid * (1.0 + gate * (1.0 - sigmoid))).astype(BF16)
    up_rows = (back * silu).astype(BF16)
    gate_out[...] = gate_rows
    up_out[...] = up_rows
    second = mm(gate_rows, gate_weight) + mm(up_rows, up_weight)
    own_out[...] = second[:row_count]
    send_out[...] = second[row_count:].astype(BF16)


def feed_grads_body(hidden, kinds, *refs):
    lefts, right_refs = refs[:kinds], refs[kinds : kinds + 2]
    sent_out, kept_out = refs[kinds + 2 :]
    right = jnp.concatenate([right_refs[0][...], right_refs[1][...]], axis=0)
    half = lefts[0].shape[1] // 2
    for kind, left_ref in enumerate(lefts):
        left = left_ref[...]
        total = mm(left[:, half:], right, TN)
        for slot in range(half // hidden):
            store_packed(
                sent_out,
                (slot * kinds + kind) * packed_rows(hidden),
                total[slot * hidden : (slot + 1) * hidden],
            )
        total = mm(left[:, :half], right, TN)
        for slot in range(half // hidden):
            at = (slot * kinds + kind) * hidden
            kept_out[at : at + hidden, :] = total[slot * hidden : (slot + 1) * hidden]


def result_body(hidden, hidden_ref, *refs):
    own_out, send_out = refs[-2:]
    row_count = own_out.shape[0]
    weights = load_packed(refs[:-2], packed_rows(hidden), 0, hidden)
    result = mm(hidden_ref[...], weights)
    own_out[...] = result[:row_count]
    send_out[...] = result[row_count:].astype(BF16)


def attend_back_body(pad, pieces, blocks, own_ref, got_ref, middle_ref, grad_ref, gains_ref, query_ref,
                     key_seg_ref, query_seg_ref, feature_ref, lse_ref, cos_ref, sin_ref, *refs):
    outs = refs[pieces + blocks :]
    query_out, rows_out, middle_grad_out, gain_out = outs[:4]
    block_outs = outs[4:]
    row_count = query_ref.shape[0]
    width = query_ref.shape[1]
    second_back = own_ref[...] + got_ref[...].astype(F32)
    middle = middle_ref[...]
    inverse = inverse_norm(middle)
    normed = middle * inverse
    gain_out[...] = jnp.broadcast_to(
        jnp.sum(second_back * normed, axis=0, keepdims=True), gain_out.shape
    )
    scaled = second_back * gains_ref[1:2, :]
    middle_grad = grad_ref[...].astype(F32) + inverse * (
        scaled - normed * jnp.mean(scaled * normed, axis=-1, keepdims=True)
    )
    middle_grad_out[...] = middle_grad
    attn_rows = middle_grad.astype(BF16)
    rows_out[...] = attn_rows
    by_slot = mm(attn_rows, load_pair(refs[:pieces], 9 * pad, pad, 1), NT).astype(BF16)
    rows = mm(by_slot, placed(feature_ref[...], width), NT).astype(BF16)

    allowed = allowed_pairs(key_seg_ref[...], query_seg_ref[...], row_count)
    joined = stacked(refs[pieces : pieces + blocks])
    queries = query_ref[...]
    query_parts, key_parts, value_parts = [], [], []
    for group in range(KVH):
        keys = joined[:, group * HD : (group + 1) * HD]
        values = joined[:, KVW + group * HD : KVW + (group + 1) * HD]
        key_sum, value_sum = None, None
        for head in range(group * GROUP, (group + 1) * GROUP):
            head_query = queries[:, head * HD : (head + 1) * HD]
            head_rows = rows[:, head * HD : (head + 1) * HD]
            scores = jnp.where(allowed, mm(keys, head_query, NT) * SCALE, MASKED_SCORE)
            exact = jnp.exp(scores - lse_ref[head : head + 1, :])
            dp = mm(values, head_rows, NT)
            weighted = exact * dp
            delta = jnp.sum(weighted, axis=0, keepdims=True)
            score_rows = (weighted - exact * delta).astype(BF16)
            query_parts.append(mm(score_rows, keys, TN) * SCALE)
            key_term = mm(score_rows, head_query)
            value_term = mm(exact.astype(BF16), head_rows)
            key_sum = key_term if key_sum is None else key_sum + key_term
            value_sum = value_term if value_sum is None else value_sum + value_term
        key_parts.append(key_sum * SCALE)
        value_parts.append(value_sum)
    joined_sum = jnp.concatenate(key_parts + value_parts, axis=1)
    for index, ref in enumerate(block_outs):
        ref[...] = joined_sum[index * row_count : (index + 1) * row_count].astype(ref.dtype)
    query_sum = jnp.concatenate(query_parts, axis=1)
    query_out[...] = turn_lanes(query_sum, cos_ref[...], -sin_ref[...]).astype(BF16)


def canonical(value, place):
    high = value.astype(BF16)
    low = (value - high.astype(F32)).astype(BF16)
    return mm(high, place, NT) + mm(low, place, NT)


def qo_grads_body(pad, act_ref, act_output_ref, query_ref, rows_ref, *refs):
    sent_out, query_kept, output_kept, back_out = refs[-4:]
    half = act_ref.shape[1] // 2
    lefts = ((act_ref[...], query_ref[...]), (act_output_ref[...], rows_ref[...]))
    sent = [mm(act[:, half:], rows, TN) for act, rows in lefts]
    for slot in range(half // pad):
        part = slice(slot * pad, (slot + 1) * pad)
        store_pair(sent_out, slot * 9 * pad, pad, sent[0][part], sent[1][part])
    for (act, rows), out in zip(lefts, (query_kept, output_kept)):
        out[...] = mm(act[:, :half], rows, TN)
    back_out[...] = mm(query_ref[...], load_pair(refs[:-4], 9 * pad, pad, 0), NT)


def kv_grads_body(shard, pad, pieces, blocks, act_ref, feature_ref, owner_ref, cos_ref, sin_ref,
                  back_ref, tok_ref, middle_grad_ref, gains_ref, second_gain_ref, *refs):
    weights = stacked(refs[:pieces])
    parts = refs[pieces : pieces + blocks]
    sent_out, kept_out, grad_out = refs[pieces + blocks :]
    width = tok_ref.shape[1]
    total = parts[0][...]
    for part in parts[1:]:
        total = total + part[...].astype(F32)
    turned = turn_lanes(total, cos_ref[...], -sin_ref[...])
    lane = lax.broadcasted_iota(jnp.int32, total.shape, 1)
    rows = jnp.where(lane < KVW, turned, total).astype(BF16)
    back = canonical(back_ref[...] + mm(rows, weights, NT), placed(feature_ref[...], width))
    source = tok_ref[...].astype(F32)
    inverse = inverse_norm(source)
    normed = source * inverse
    first_gain = jnp.sum(back * normed, axis=0, keepdims=True)
    slots = owner_ref.shape[0]
    spread = spread_lanes(shard, 2 * KVW, width)
    mine = owner_ref[...] == lax.broadcasted_iota(jnp.int32, (slots, width), 1) // shard
    place_at = lax.broadcasted_iota(jnp.int32, (slots, slots * pad), 1)
    slot_at = lax.broadcasted_iota(jnp.int32, (slots, slots * pad), 0)
    extra = None
    for index, gain in enumerate((first_gain, second_gain_ref[0:1, :])):
        by_slot = mm(jnp.where(mine, gain, 0.0).astype(BF16), spread, NT).astype(BF16)
        pick = jnp.where(place_at == slot_at * pad + shard + index, 1.0, 0.0).astype(BF16)
        term = mm(pick, by_slot, TN)
        extra = term if extra is None else extra + term
    grads = mm(act_ref[...], rows, TN) + extra
    half = grads.shape[0] // 2
    sent_out[...] = grads[half:].astype(BF16)
    kept_out[...] = grads[:half]
    scaled = back * gains_ref[0:1, :]
    input_grad = middle_grad_ref[...] + inverse * (
        scaled - normed * jnp.mean(scaled * normed, axis=-1, keepdims=True)
    )
    grad_out[...] = jnp.transpose(input_grad)


def core_sum_body(pad, query_ref, output_ref, qo_got, kv_ref, kv_got, sent_out, query_out,
                  output_out, kv_out):
    query = query_ref[...] + load_pair([qo_got], 9 * pad, pad, 0).astype(F32)
    output = output_ref[...] + load_pair([qo_got], 9 * pad, pad, 1).astype(F32)
    kv = kv_ref[...] + kv_got[...].astype(F32)
    half = query.shape[0] // 2
    query_out[...] = query[:half]
    output_out[...] = output[:half]
    kv_out[...] = kv[:half]
    for slot in range(half // pad):
        part = slice(half + slot * pad, half + (slot + 1) * pad)
        store_pair(sent_out, slot * 12 * pad, pad, query[part], output[part])
        store_three(sent_out, slot * 12 * pad + 9 * pad, pad, kv[part])


def x_sum_body(pad, query_ref, output_ref, kv_ref, got_ref, *outs):
    query = query_ref[...] + load_pair([got_ref], 12 * pad, pad, 0).astype(F32)
    output = output_ref[...] + load_pair([got_ref], 12 * pad, pad, 1).astype(F32)
    kv = kv_ref[...] + load_three([got_ref], 12 * pad, 9 * pad, pad).astype(F32)
    for slot, out in enumerate(outs):
        part = slice(slot * pad, (slot + 1) * pad)
        store_pair(out, 0, pad, query[part], output[part])
        store_three(out, 9 * pad, pad, kv[part])


def feed_sum_body(hidden, kinds, kept_ref, got_ref, *outs):
    size = packed_rows(hidden)
    for slot, out in enumerate(outs):
        for kind in range(kinds):
            at = slot * kinds + kind
            got = load_packed([got_ref.at[pl.ds(at * size, size), :]], size, 0, hidden)
            total = kept_ref[at * hidden : (at + 1) * hidden, :] + got.astype(F32)
            store_packed(out, kind * size, total)


def total_body(*refs):
    total = refs[0][...]
    for ref in refs[1:-1]:
        total = total + ref[...].astype(F32)
    refs[-1][...] = total.astype(BF16)


def two_copies(own_ref, got_ref):
    return own_ref[...].astype(F32) + got_ref[...].astype(F32)


def copies_total(shard, pad, hidden, down_refs, feed_refs, rest_refs):
    size = packed_rows(hidden)
    down = two_copies_packed(down_refs, size, 0, hidden)
    gate = two_copies_packed(feed_refs, 2 * size, 0, hidden)
    up = two_copies_packed(feed_refs, 2 * size, size, hidden)
    own, got = rest_refs
    query = sum(load_pair([ref], 12 * pad, pad, 0).astype(F32) for ref in rest_refs)
    output = sum(load_pair([ref], 12 * pad, pad, 1).astype(F32) for ref in rest_refs)
    kv = sum(load_three([ref], 12 * pad, 9 * pad, pad).astype(F32) for ref in rest_refs)
    return (
        query[:shard],
        kv[:shard, :KVW],
        kv[:shard, KVW:],
        output[:shard],
        gate,
        up,
        down,
        kv[shard : shard + 2, :shard],
    )


def two_copies_packed(refs, slot_rows, base, rows):
    return sum(load_packed([ref], slot_rows, base, rows).astype(F32) for ref in refs)


def moment_messages_body(shard, pad, hidden, stride, at_ref, down_ref, down_got, feed_ref, feed_got,
                         rest_ref, rest_got, query_ref, key_ref, value_ref, output_ref, gate_ref,
                         up_ref, down_moment_ref, *refs):
    outs, scratch = refs[:-1], refs[-1]
    scratch[...] = jnp.zeros(scratch.shape, BF16)
    totals = copies_total(
        shard, pad, hidden, (down_ref, down_got), (feed_ref, feed_got), (rest_ref, rest_got)
    )
    moments = [
        MOMENTUM * ref[...] + total
        for ref, total in zip(
            (query_ref, key_ref, value_ref, output_ref, gate_ref, up_ref, down_moment_ref), totals
        )
    ]
    for group, value in enumerate(moments[4:]):
        store_packed(scratch.at[group], 0, value)
    target = scratch.at[3]
    for which, value in enumerate((moments[0], moments[3])):
        for index in range(FULL):
            at = (which * FULL + index) * pad
            target[at : at + shard, :] = value[:, index * 128 : (index + 1) * 128].astype(BF16)
        at = 2 * FULL * pad
        target[at : at + shard, which * 64 : which * 64 + 64] = value[:, FULL * 128 :].astype(BF16)
    kv = jnp.concatenate([moments[1], moments[2]], axis=1)
    for index in range(3):
        at = (9 + index) * pad
        target[at : at + shard, :] = kv[:, index * 128 : (index + 1) * 128].astype(BF16)
    for other, out in enumerate(outs):
        out[...] = scratch[(at_ref[0] ^ other) // stride]


def moments_body(shard, pad, hidden, down_ref, down_got, feed_ref, feed_got, rest_ref, rest_got,
                 middle_ref, result_ref, result_got, *refs):
    moments, grads, news, out_tokens = refs[:8], refs[8:16], refs[16:24], refs[24]
    totals = copies_total(
        shard, pad, hidden, (down_ref, down_got), (feed_ref, feed_got), (rest_ref, rest_got)
    )
    for moment, total, grad, new in zip(moments, totals, grads, news):
        grad[...] = total
        new[...] = MOMENTUM * moment[...] + total
    result = middle_ref[...] + result_ref[...] + result_got[...].astype(F32)
    out_tokens[...] = jnp.transpose(result).astype(BF16)


def polar_steps(wide_ref):
    size = wide_ref.shape[0]
    first = wide_ref[...]
    norm = jnp.sqrt(jnp.sum(first * first)) + NORM_FLOOR
    wide_ref[...] = first / norm

    def step(index, carry):
        row = lax.broadcasted_iota(jnp.int32, (size, size), 0)
        col = lax.broadcasted_iota(jnp.int32, (size, size), 1)
        diagonal = row == col
        rounded = wide_ref[...].astype(BF16)
        gram = mm(rounded, rounded, NT)
        mean = jnp.sum(jnp.where(diagonal, gram, 0.0)) / size
        rest = gram - jnp.where(diagonal, mean, 0.0)
        rest_rounded = rest.astype(BF16)
        square = mm(rest_rounded, rest_rounded) + (2.0 * mean) * rest
        square = square + jnp.where(diagonal, mean * mean, 0.0)
        poly = CUBIC_TERM * gram + QUINTIC_TERM * square
        shift = jnp.sum(jnp.where(diagonal, poly, 0.0)) / size
        poly_rest = (poly - jnp.where(diagonal, shift, 0.0)).astype(BF16)
        wide_ref[...] = (LINEAR_TERM + shift) * wide_ref[...] + mm(poly_rest, rounded)
        return carry

    lax.fori_loop(0, NS_STEPS, step, 0)


def big_body(pad, hidden, slot_rows, pieces, at_ref, *refs):
    outs, wide_ref = refs[pieces:-2], refs[-2]
    tall = load_packed(refs[:pieces], slot_rows, 0, hidden)
    wide_ref[...] = jnp.transpose(tall.astype(F32))
    polar_steps(wide_ref)
    result = jnp.transpose(wide_ref[:, : len(outs) * hidden])
    for slot, out in enumerate(outs):
        if packed_rows(hidden) < out.shape[0]:
            out[...] = jnp.zeros(out.shape, BF16)
        store_packed(out, 0, result[slot * hidden : (slot + 1) * hidden])


def small_body(pad, hidden, slot_rows, pieces, at_ref, *refs):
    outs, large_ref, little_ref = refs[pieces:-2], refs[-2], refs[-1]
    ins = refs[:pieces]
    core = at_ref[1]
    large = jnp.where(
        core == 0,
        load_pair(ins, slot_rows, pad, 0).astype(F32),
        load_pair(ins, slot_rows, pad, 1).astype(F32),
    )
    little = load_three(ins, slot_rows, 9 * pad, pad).astype(F32)
    little = jnp.where(core == 0, little[:, :KVW], little[:, KVW : 2 * KVW])
    count = large.shape[0]
    large_ref[:, :count] = jnp.transpose(large)
    little_ref[...] = jnp.transpose(little)
    polar_steps(large_ref.at[:, :count])
    polar_steps(little_ref)
    large = jnp.transpose(large_ref[:, :count])
    little = jnp.transpose(little_ref[...])
    other = count // 2
    for slot, out in enumerate(outs):
        if 12 * pad < out.shape[0]:
            out[...] = jnp.zeros(out.shape, BF16)
        own = slice(slot * pad, (slot + 1) * pad)
        cross = slice(other + slot * pad, other + (slot + 1) * pad)
        store_pair(out, 0, pad, large[own], large[cross])
        store_three(
            out, 9 * pad, pad, jnp.concatenate([little[own], little[cross]], axis=1)
        )


def pick_body(stride, at_ref, *refs):
    answers, out = refs[:-1], refs[-1]
    for other, ref in enumerate(answers):

        @pl.when(at_ref[0] ^ other == 3 * stride)
        def _():
            out[...] = ref[...]


def weights_body(shard, pad, hidden, stride, factors, at_ref, *refs):
    count = len(refs) - 1 - 2 - 8 - 16
    answers = refs[:count]
    cross_ref, gain_moment_ref = refs[count : count + 2]
    masters = refs[count + 2 : count + 10]
    news, rounded = refs[count + 10 : count + 18], refs[count + 18 : count + 26]
    scratch = refs[-1]
    for group in range(4):
        for other, ref in enumerate(answers):

            @pl.when(at_ref[0] ^ other == group * stride)
            def _():
                scratch[group] = ref[...]

    core = at_ref[1]
    target = scratch.at[3]
    rows = target.shape[0]
    own_large = load_pair([target], rows, pad, 0)[:shard].astype(F32)
    other_large = load_pair([cross_ref], rows, pad, 1)[:shard].astype(F32)
    own_little = load_three([target], rows, 9 * pad, pad)[:shard, :KVW].astype(F32)
    other_little = load_three([cross_ref], rows, 9 * pad, pad)[:shard, KVW:].astype(F32)
    first = core == 0
    polars = (
        jnp.where(first, own_large, other_large),
        jnp.where(first, own_little, other_little),
        jnp.where(first, other_little, own_little),
        jnp.where(first, other_large, own_large),
    ) + tuple(
        load_packed([scratch.at[group]], rows, 0, hidden).astype(F32) for group in range(3)
    )
    for master, polar, factor, new, low in zip(masters, polars, factors, news, rounded):
        weight = master[...] - factor * polar
        new[...] = weight
        low[...] = weight.astype(BF16)
    weight = masters[7][...] - GAIN_RATE * gain_moment_ref[...]
    news[7][...] = weight
    rounded[7][...] = weight.astype(BF16)


def local(
    tokens,
    out_grad,
    segments,
    query_copy,
    key_copy,
    value_copy,
    output_copy,
    gate_copy,
    up_copy,
    down_copy,
    gains_copy,
    query_master,
    key_master,
    value_master,
    output_master,
    gate_master,
    up_master,
    down_master,
    gains_master,
    query_moment,
    key_moment,
    value_moment,
    output_moment,
    gate_moment,
    up_moment,
    down_moment,
    gains_moment,
):
    x_size, z_size = lax.axis_size("x"), lax.axis_size("ctx")
    x_at, core_at, z_at = lax.axis_index("x"), lax.axis_index("core"), lax.axis_index("ctx")
    if z_size % 4:
        raise ValueError("ctx size")
    stride = z_size // 4
    slots = 2 * x_size * z_size
    rows, width = tokens.shape[1], tokens.shape[2]
    shard = query_copy.shape[0]
    pad = -(-(shard + 2) // 8) * 8
    hidden = down_copy.shape[0]
    back_blocks = z_size // 2
    blocks = back_blocks + 1
    at = jnp.stack([z_at, core_at, lax.axis_index("rep")]).astype(jnp.int32)
    bind = functools.partial

    def join(parts):
        total = sum(part.shape[0] for part in parts)
        return call(join_body, shaped(parts[0].dtype, total, parts[0].shape[1]), *parts)

    def along_ctx(value):
        return join([value] + [flip(value, "ctx", other) for other in range(1, z_size)])

    def along_x(pieces):
        for bit in bits_of(x_size):
            pieces = pieces + [flip(piece, "x", bit) for piece in pieces]
        return pieces

    def along_core(pieces):
        return pieces + [flip(piece, "core", 1) for piece in pieces]

    kv_message = call(
        bind(kv_message_body, shard), shaped(BF16, pad, 2 * KVW), key_copy, value_copy, gains_copy
    )
    kv_joined = along_ctx(kv_message)
    frequency = np.float32(ROPE_BASE) ** (
        np.float32(-2.0) * (np.arange(128) % (HD // 2)).astype(np.float32) / np.float32(HD)
    )
    tok, grad, cosine, sine, key_seg, query_seg = call(
        bind(setup_body, blocks),
        (
            shaped(BF16, rows, width),
            shaped(BF16, rows, width),
            shaped(F32, rows, 128),
            shaped(F32, rows, 128),
            shaped(F32, blocks * rows, 1),
            shaped(F32, 1, rows),
        ),
        at,
        tokens[0].T,
        out_grad[0].T,
        segments.reshape(z_size, rows),
        jnp.asarray(frequency[None, :], F32),
        scalars=1,
    )
    qo_message = call(
        bind(qo_message_body, shard, pad),
        shaped(BF16, 9 * pad, 128),
        query_copy,
        output_copy,
        after=(kv_joined,),
    )
    size = packed_rows(hidden)
    feed_message = call(
        feed_message_body,
        shaped(BF16, size, 128),
        at,
        gate_copy.T,
        up_copy.T,
        scalars=1,
        after=(qo_message,),
    )
    kv_pieces = along_core(along_x([kv_joined]))
    qo_pieces = along_core(along_x([along_ctx(qo_message)]))
    other_grad = flip(grad, "core", 1)
    pieces = len(kv_pieces)

    def device_of(position):
        z_part = z_at ^ (position % z_size)
        x_part = x_at ^ (position // z_size % x_size)
        core_part = core_at ^ (position // (z_size * x_size))
        return (x_part * 2 + core_part) * z_size + z_part

    column = lax.broadcasted_iota(jnp.int32, (1, slots * pad), 1)
    inside = column % pad
    feature = jnp.where(inside < shard, device_of(column // pad) * shard + inside, -1)
    owner = device_of(lax.broadcasted_iota(jnp.int32, (slots, 1), 0))

    kv_own, act_first, act_slots, gains = call(
        bind(kv_body, shard, pad, pieces),
        (
            shaped(BF16, rows, 2 * KVW),
            shaped(BF16, rows, width),
            shaped(BF16, rows, slots * pad),
            shaped(F32, 8, width),
        ),
        tok,
        feature,
        owner,
        cosine,
        sine,
        *kv_pieces,
    )
    kv_blocks = [kv_own]
    for back in range(1, blocks):
        pairs = [(i, i + back) for i in range(z_size - back)]
        kv_blocks.append(lax.ppermute(kv_own, "ctx", pairs))
    down_message = call(
        down_message_body, shaped(BF16, size, 128), down_copy, after=(kv_own,)
    )
    mine_pieces = along_x([along_ctx(feed_message)])
    copied_pieces = [flip(piece, "rep", 1) for piece in mine_pieces]
    down_pieces = along_x([along_ctx(down_message)])
    feed_pieces = len(down_pieces)
    queries = call(
        bind(query_body, pad), shaped(BF16, rows, width), act_slots, cosine, sine, *qo_pieces
    )
    lse, act_output, middle, act_second = call(
        bind(attend_body, pad, pieces, blocks),
        (
            shaped(F32, H, rows),
            shaped(BF16, rows, slots * pad),
            shaped(F32, rows, width),
            shaped(BF16, rows, width),
        ),
        queries,
        key_seg,
        query_seg,
        feature,
        tok,
        gains,
        *qo_pieces,
        *kv_blocks,
    )

    other_act = flip(act_second, "core", 1)
    inner = slots // 2 * hidden
    hidden_rows, gate_rows, up_rows, second_own, second_send = call(
        bind(feed_body, hidden, feed_pieces),
        (shaped(BF16, 2 * rows, inner),) * 3
        + (shaped(F32, rows, width), shaped(BF16, rows, width)),
        at,
        act_second,
        other_act,
        grad,
        other_grad,
        *mine_pieces,
        *copied_pieces,
        *down_pieces,
        scalars=1,
    )
    second_got = flip(second_send, "core", 1)
    kept_slots = slots // 4

    def feed_gradients(lefts, rights, after=()):
        kinds = len(lefts)
        sent, kept = call(
            bind(feed_grads_body, hidden, kinds),
            (
                shaped(BF16, kept_slots * kinds * size, 128),
                shaped(F32, kept_slots * kinds * hidden, width),
            ),
            *lefts,
            *rights,
            after=after,
        )
        return sent, kept, flip(sent, "x", 1)

    def feed_totals(kinds, kept, got, after=()):
        parts = call(
            bind(feed_sum_body, hidden, kinds),
            (shaped(F32, kinds * size, 128),)
            + (shaped(BF16, kinds * size, 128),) * (z_size - 1),
            kept,
            got,
            after=after,
        )
        return [parts[0]] + [flip(parts[other], "ctx", other) for other in range(1, z_size)]

    def added(parts, after=()):
        total = call(total_body, shaped(BF16, *parts[0].shape), *parts, after=after)
        return total, flip(total, "rep", 1)

    down_sent, down_kept, down_got = feed_gradients([hidden_rows], [grad, other_grad])
    feed_sent, feed_kept, feed_got = feed_gradients(
        [gate_rows, up_rows], [act_second, other_act], (down_sent,)
    )

    outs = call(
        bind(attend_back_body, pad, pieces, blocks),
        (
            shaped(BF16, rows, width),
            shaped(BF16, rows, width),
            shaped(F32, rows, width),
            shaped(F32, 8, width),
            shaped(F32, rows, 2 * KVW),
        )
        + (shaped(BF16, rows, 2 * KVW),) * back_blocks,
        second_own,
        second_got,
        middle,
        grad,
        gains,
        queries,
        key_seg,
        query_seg,
        feature,
        lse,
        cosine,
        sine,
        *qo_pieces,
        *kv_blocks,
        after=(feed_sent,),
    )
    query_rows, attn_rows, middle_grad, second_gain = outs[:4]
    kv_terms = [outs[4]]
    for back in range(1, blocks):
        pairs = [(i + back, i) for i in range(z_size - back)]
        kv_terms.append(lax.ppermute(outs[4 + back], "ctx", pairs))
    down_parts = feed_totals(1, down_kept, down_got, (query_rows,))

    qo_sent, query_kept, output_kept, query_back = call(
        bind(qo_grads_body, pad),
        (
            shaped(BF16, slots // 2 * 9 * pad, 128),
            shaped(F32, slots // 2 * pad, width),
            shaped(F32, slots // 2 * pad, width),
            shaped(F32, rows, slots * pad),
        ),
        act_slots,
        act_output,
        query_rows,
        attn_rows,
        *qo_pieces,
    )
    qo_got = flip(qo_sent, "core", 1)
    kv_sent, kv_kept, input_grad = call(
        bind(kv_grads_body, shard, pad, pieces, blocks),
        (
            shaped(BF16, slots // 2 * pad, 2 * KVW),
            shaped(F32, slots // 2 * pad, 2 * KVW),
            shaped(F32, width, rows),
        ),
        act_slots,
        feature,
        owner,
        cosine,
        sine,
        query_back,
        tok,
        middle_grad,
        gains,
        second_gain,
        *kv_pieces,
        *kv_terms,
        after=(down_parts[0],),
    )
    kv_got = flip(kv_sent, "core", 1)
    feed_parts = feed_totals(2, feed_kept, feed_got, (kv_sent,))
    rest_sent, query_kept, output_kept, kv_kept = call(
        bind(core_sum_body, pad),
        (
            shaped(BF16, kept_slots * 12 * pad, 128),
            shaped(F32, kept_slots * pad, width),
            shaped(F32, kept_slots * pad, width),
            shaped(F32, kept_slots * pad, 2 * KVW),
        ),
        query_kept,
        output_kept,
        qo_got,
        kv_kept,
        kv_got,
    )
    rest_got = flip(rest_sent, "x", 1)
    down_total, down_copied = added(down_parts, (rest_sent,))
    result_own, result_send = call(
        bind(result_body, hidden),
        (shaped(F32, rows, width), shaped(BF16, rows, width)),
        hidden_rows,
        *down_pieces,
        after=(rest_sent,),
    )
    result_got = flip(result_send, "core", 1)
    rest_parts = call(
        bind(x_sum_body, pad),
        (shaped(F32, 12 * pad, 128),) + (shaped(BF16, 12 * pad, 128),) * (z_size - 1),
        query_kept,
        output_kept,
        kv_kept,
        rest_got,
    )
    rest_parts = [rest_parts[0]] + [
        flip(rest_parts[other], "ctx", other) for other in range(1, z_size)
    ]
    feed_total, feed_copied = added(feed_parts)
    rest_total, rest_copied = added(rest_parts)

    slot_rows = max(size, 12 * pad)
    message = shaped(BF16, slot_rows, 128)
    sums = (down_total, down_copied, feed_total, feed_copied, rest_total, rest_copied)
    natural = (
        query_moment,
        key_moment,
        value_moment,
        output_moment,
        gate_moment.T,
        up_moment.T,
        down_moment,
        gains_moment,
    )
    messages = call(
        bind(moment_messages_body, shard, pad, hidden, stride),
        (message,) * z_size,
        at,
        *sums,
        *natural[:7],
        scratch=[pltpu.VMEM((4, slot_rows, 128), BF16)],
        scalars=1,
    )
    owner_columns = [g * stride for g in range(4)]
    arrived = [messages[0]]
    for other in range(1, z_size):
        pairs = [(d ^ other, d) for d in owner_columns]
        arrived.append(lax.ppermute(messages[other], "ctx", pairs))
    matrix_pieces = along_core(along_x([join(arrived)]))
    moment_types = tuple(shaped(F32, *value.shape) for value in natural)
    outs = call(
        bind(moments_body, shard, pad, hidden),
        moment_types * 2 + (shaped(BF16, width, rows),),
        *sums,
        middle,
        result_own,
        result_got,
        *natural,
        after=(messages[0],),
    )
    totals, new_moments, out_tokens = list(outs[:8]), list(outs[8:16]), outs[16]

    large_lanes = max(hidden, pad) * slots

    def solver(body):
        def run(at, *parts):
            return call(
                bind(body, pad, hidden, slot_rows, pieces),
                (message,) * z_size,
                at,
                *parts,
                scratch=[
                    pltpu.VMEM((width, large_lanes), F32),
                    pltpu.VMEM((KVW, slots * pad), F32),
                ],
                scalars=1,
            )

        return run

    solved = lax.cond(
        z_at // stride == 3, solver(small_body), solver(big_body), at, *matrix_pieces
    )
    answers = [solved[0]]
    for other in range(1, z_size):
        pairs = [(d, d ^ other) for d in owner_columns]
        answers.append(lax.ppermute(solved[other], "ctx", pairs))
    picked = call(bind(pick_body, stride), message, at, *answers, scalars=1)
    crossed = flip(picked, "core", 1)
    masters = (
        query_master,
        key_master,
        value_master,
        output_master,
        gate_master.T,
        up_master.T,
        down_master,
        gains_master,
    )
    full = slots * hidden
    full_shapes = (
        (width, width),
        (width, KVW),
        (width, KVW),
        (width, width),
        (width, full),
        (width, full),
        (full, width),
    )
    factors = [STEP_SIZE * math.sqrt(max(shape) / shape[0]) for shape in full_shapes]
    outs = call(
        bind(weights_body, shard, pad, hidden, stride, factors),
        tuple(shaped(F32, *value.shape) for value in masters)
        + tuple(shaped(BF16, *value.shape) for value in masters),
        at,
        *answers,
        crossed,
        new_moments[7],
        *masters,
        scratch=[pltpu.VMEM((4, slot_rows, 128), BF16)],
        scalars=1,
    )
    weights, rounded = list(outs[:8]), list(outs[8:])
    for values in (totals, new_moments, weights, rounded):
        for index in (4, 5):
            values[index] = values[index].T
    return (out_tokens.T[None], input_grad.T[None], *totals, *new_moments, *weights, *rounded)


def solution(mesh):
    dp_size, ctx_size, rep_size = (mesh.shape[name] for name in ("dp", "ctx", "rep"))
    split = Mesh(
        mesh.devices.reshape(dp_size // 2, 2, ctx_size, rep_size), ("x", "core", "ctx", "rep")
    )
    batch = ("x", "core", "rep")
    parts = ("x", "core", "ctx")
    by_row, by_column = P(parts, None), P(None, parts)
    weights = (by_row, by_row, by_row, by_row, by_column, by_column, by_row, by_column)
    token_spec = P(batch, "ctx", None)
    return jax.shard_map(
        local,
        mesh=split,
        in_specs=(token_spec, token_spec, P(batch, None)) + weights * 3,
        out_specs=(token_spec, token_spec) + weights * 4,
        check_vma=False,
    )
```

```python
import functools
import math

import jax
import jax.numpy as jnp
import numpy as np
from jax import lax
from jax.experimental import pallas as pl
from jax.experimental.pallas import tpu as pltpu
from jax.sharding import Mesh
from jax.sharding import PartitionSpec as P


H = 9
KVH = 3
HD = 64
GROUP = H // KVH
KVW = KVH * HD
NS_STEPS = 5

EPSILON = 1e-05
ROPE_BASE = 10000.0
MASKED_SCORE = -1e30
MOMENTUM = 0.5
STEP_SIZE = 0.5
GAIN_RATE = 0.001
LINEAR_TERM = 3.4445
CUBIC_TERM = -4.775
QUINTIC_TERM = 2.0315
NORM_FLOOR = 1e-07
SCALE = HD ** (-0.5)

F32 = jnp.float32
BF16 = jnp.bfloat16


NN = (((1,), (0,)), ((), ()))
NT = (((1,), (1,)), ((), ()))
TN = (((0,), (0,)), ((), ()))


def mm(left, right, dims=NN):
    return lax.dot_general(left, right, dims, preferred_element_type=F32)


def flip(value, axis, bit):
    return lax.ppermute(value, axis, [(i, i ^ bit) for i in range(lax.axis_size(axis))])


def bits_of(size):
    bits = []
    while size > 1:
        size //= 2
        bits.append(size)
    return bits


def call(body, out_shape, *operands, scratch=(), scalars=0):
    specs = [pl.BlockSpec(memory_space=pltpu.SMEM)] * scalars
    specs += [pl.BlockSpec(memory_space=pltpu.VMEM)] * (len(operands) - scalars)
    return pl.pallas_call(
        body,
        out_shape=out_shape,
        in_specs=specs,
        scratch_shapes=scratch,
        compiler_params=pltpu.CompilerParams(vmem_limit_bytes=56 * 1024 * 1024),
    )(*operands)


def shaped(dtype, *shape):
    return jax.ShapeDtypeStruct(shape, dtype)


def turn_chunk(chunk, cosine, sine):
    lane = lax.broadcasted_iota(jnp.int32, chunk.shape, 1)
    turned = jnp.where(
        lane % HD < HD // 2,
        pltpu.roll(chunk, 128 - HD // 2, 1),
        pltpu.roll(chunk, HD // 2, 1),
    )
    return chunk * cosine + turned * sine


def turn_lanes(full, cosine, sine):
    width = full.shape[1]
    pieces = []
    for start in range(0, width - width % 128, 128):
        pieces.append(turn_chunk(full[:, start : start + 128], cosine, sine))
    if width % 128:
        last = full[:, width - 64 :]
        pieces.append(turn_chunk(jnp.concatenate([last, last], axis=1), cosine, sine)[:, :64])
    return jnp.concatenate(pieces, axis=1)


def allowed_pairs(key_seg, query_seg, row_count):
    shape = (key_seg.shape[0], query_seg.shape[1])
    key_row = lax.broadcasted_iota(jnp.int32, shape, 0)
    query_col = lax.broadcasted_iota(jnp.int32, shape, 1)
    earlier = (key_row >= row_count) | (key_row <= query_col)
    return (key_seg == query_seg) & earlier


def placed(feature, width):
    at = lax.broadcasted_iota(jnp.int32, (width, feature.shape[1]), 0)
    return jnp.where(at == feature, 1.0, 0.0).astype(BF16)


def stacked(refs):
    return jnp.concatenate([ref[...] for ref in refs], axis=0)


def inverse_norm(value):
    return lax.rsqrt(jnp.mean(value * value, axis=-1, keepdims=True) + EPSILON)


FULL = 4


def cut(rows):
    return min(rows, -(-((rows + 1) // 2) // 16) * 16)


def packed_rows(rows):
    return FULL * rows + cut(rows)


def store_packed(out, base, value):
    rows, dtype = value.shape[0], out.dtype
    low = cut(rows)
    for index in range(FULL):
        at = base + index * rows
        out[at : at + rows, :] = value[:, index * 128 : (index + 1) * 128].astype(dtype)
    at = base + FULL * rows
    out[at : at + low, 0:64] = value[:low, FULL * 128 :].astype(dtype)
    if rows - low < low:
        out[at : at + low, 64:128] = jnp.zeros((low, 64), dtype)
    if rows > low:
        out[at : at + rows - low, 64:128] = value[low:, FULL * 128 :].astype(dtype)


def load_packed(refs, slot_rows, base, rows):
    places = [(ref, at + base) for ref in refs for at in range(0, ref.shape[0], slot_rows)]
    low = cut(rows)
    columns = []
    for index in range(FULL):
        columns.append(
            jnp.concatenate(
                [ref[at + index * rows : at + (index + 1) * rows, :] for ref, at in places], axis=0
            )
        )
    rest = []
    for ref, at in places:
        first = at + FULL * rows
        rest.append(ref[first : first + low, 0:64])
        if rows > low:
            rest.append(ref[first : first + rows - low, 64:128])
    columns.append(jnp.concatenate(rest, axis=0))
    return jnp.concatenate(columns, axis=1)


def store_pair(out, base, pad, first, second):
    for which, value in enumerate((first, second)):
        for index in range(FULL):
            at = base + (which * FULL + index) * pad
            out[at : at + pad, :] = value[:, index * 128 : (index + 1) * 128].astype(out.dtype)
        at = base + 2 * FULL * pad
        out[at : at + pad, which * 64 : which * 64 + 64] = value[:, FULL * 128 :].astype(out.dtype)


def load_pair(refs, slot_rows, pad, which):
    places = [(ref, at) for ref in refs for at in range(0, ref.shape[0], slot_rows)]
    columns = []
    for index in range(FULL):
        first = (which * FULL + index) * pad
        columns.append(
            jnp.concatenate([ref[at + first : at + first + pad, :] for ref, at in places], axis=0)
        )
    first = 2 * FULL * pad
    columns.append(
        jnp.concatenate(
            [
                ref[at + first : at + first + pad, which * 64 : which * 64 + 64]
                for ref, at in places
            ],
            axis=0,
        )
    )
    return jnp.concatenate(columns, axis=1)


def store_three(out, base, pad, value):
    for index in range(3):
        at = base + index * pad
        out[at : at + pad, :] = value[:, index * 128 : (index + 1) * 128].astype(out.dtype)


def load_three(refs, slot_rows, base, pad):
    places = [(ref, at + base) for ref in refs for at in range(0, ref.shape[0], slot_rows)]
    columns = [
        jnp.concatenate(
            [ref[at + index * pad : at + (index + 1) * pad, :] for ref, at in places], axis=0
        )
        for index in range(3)
    ]
    return jnp.concatenate(columns, axis=1)


def kv_message_body(shard, key_ref, value_ref, gains_ref, out_ref):
    out_ref[...] = jnp.zeros(out_ref.shape, BF16)
    out_ref[0:shard, 0:KVW] = key_ref[...]
    out_ref[0:shard, KVW : 2 * KVW] = value_ref[...]
    out_ref[shard : shard + 2, 0:shard] = gains_ref[...]


def qo_message_body(shard, pad, query_ref, output_ref, out_ref):
    out_ref[...] = jnp.zeros(out_ref.shape, BF16)
    for which, ref in enumerate((query_ref, output_ref)):
        for index in range(FULL):
            at = (which * FULL + index) * pad
            out_ref[at : at + shard, :] = ref[:, index * 128 : (index + 1) * 128]
        at = 2 * FULL * pad
        out_ref[at : at + shard, which * 64 : which * 64 + 64] = ref[:, FULL * 128 :]


def shard_of(position, at_ref, x_size, z_size):
    z_part = at_ref[0] ^ (position & (z_size - 1))
    x_part = at_ref[3] ^ ((position // z_size) & (x_size - 1))
    core_part = at_ref[1] ^ (position // (z_size * x_size))
    return (x_part * 2 + core_part) * z_size + z_part


def setup_body(blocks, shard, pad, x_size, z_size, at_ref, tok_ref, grad_ref, seg_ref,
               frequency_ref, tok_out, grad_out, cos_out, sin_out, key_seg_out, query_seg_out,
               feature_out, owner_out):
    rows = tok_ref.shape[1]
    tok_out[...] = jnp.transpose(tok_ref[...])
    grad_out[...] = jnp.transpose(grad_ref[...])
    z_at = at_ref[0]
    every = [seg_ref[:, block * rows : (block + 1) * rows].astype(F32) for block in range(z_size)]

    def row_of(wanted):
        row = jnp.full((1, rows), -1.0, F32)
        for block, value in enumerate(every):
            row = jnp.where(wanted == block, value, row)
        return row

    def upright(row):
        return jnp.transpose(jnp.broadcast_to(row, (8, rows)))[:, 0:1]

    own = row_of(z_at)
    own_column = upright(own)
    query_seg_out[...] = own
    key_seg_out[0:rows, :] = own_column
    for back in range(1, blocks):
        key_seg_out[back * rows : (back + 1) * rows, :] = upright(row_of(z_at - back))
    first = jnp.zeros((rows, 1), F32)
    for value in every:
        first = first + jnp.sum(jnp.where(value < own_column, 1.0, 0.0), axis=1, keepdims=True)
    index = lax.broadcasted_iota(jnp.int32, (rows, 1), 0) + z_at * rows
    angles = (index.astype(F32) - first) * frequency_ref[...]
    lane = lax.broadcasted_iota(jnp.int32, angles.shape, 1)
    cos_out[...] = jnp.cos(angles)
    sin_out[...] = jnp.sin(angles) * jnp.where(lane % HD < HD // 2, -1.0, 1.0)
    column = lax.broadcasted_iota(jnp.int32, feature_out.shape, 1)
    slot = jnp.floor((column.astype(F32) + 0.5) / pad).astype(jnp.int32)
    inside = column - slot * pad
    feature = shard_of(slot, at_ref, x_size, z_size) * shard + inside
    feature_out[...] = jnp.where(inside < shard, feature, -1)
    position = lax.broadcasted_iota(jnp.int32, owner_out.shape, 0)
    owner_out[...] = shard_of(position, at_ref, x_size, z_size)


def join_body(*refs):
    out, at = refs[-1], 0
    for ref in refs[:-1]:
        out[at : at + ref.shape[0], :] = ref[...]
        at += ref.shape[0]


def pack_body(*refs):
    out = refs[-1]
    size = packed_rows(refs[0].shape[0])
    for slot, ref in enumerate(refs[:-1]):
        store_packed(out, slot * size, ref[...])


def kv_body(shard, pad, pieces, tok_ref, feature_ref, owner_ref, cos_ref, sin_ref, *refs):
    kv_out, act_out, act_kv_out, gains_out = refs[pieces:]
    weights = stacked(refs[:pieces])
    source = tok_ref[...].astype(F32)
    width = source.shape[1]
    slots = owner_ref.shape[0]
    place_at = lax.broadcasted_iota(jnp.int32, (slots, slots * pad), 1)
    slot_at = lax.broadcasted_iota(jnp.int32, (slots, slots * pad), 0)
    spread = spread_lanes(shard, 2 * KVW, width)
    mine = owner_ref[...] == lax.broadcasted_iota(jnp.int32, (slots, width), 1) // shard
    gains_out[...] = jnp.zeros(gains_out.shape, F32)
    for index in range(2):
        pick = jnp.where(place_at == slot_at * pad + shard + index, 1.0, 0.0).astype(BF16)
        by_slot = mm(pick, weights).astype(BF16)
        gain = jnp.sum(jnp.where(mine, mm(by_slot, spread), 0.0), axis=0, keepdims=True)
        gains_out[index : index + 1, :] = gain
    act = (source * inverse_norm(source) * gains_out[0:1, :]).astype(BF16)
    act_out[...] = act
    act_kv = mm(act, placed(feature_ref[...], width)).astype(BF16)
    act_kv_out[...] = act_kv
    pre = mm(act_kv, weights)
    turned = turn_lanes(pre, cos_ref[...], sin_ref[...])
    lane = lax.broadcasted_iota(jnp.int32, pre.shape, 1)
    kv_out[...] = jnp.where(lane < KVW, turned, pre).astype(BF16)


def spread_lanes(shard, lanes, width):
    lane = lax.broadcasted_iota(jnp.int32, (lanes, width), 0)
    feature = lax.broadcasted_iota(jnp.int32, (lanes, width), 1)
    return jnp.where((feature % shard == lane) & (lane < shard), 1.0, 0.0).astype(BF16)


def query_body(pad, act_ref, cos_ref, sin_ref, *refs):
    weights = load_pair(refs[:-1], 9 * pad, pad, 0)
    pre = mm(act_ref[...], weights)
    refs[-1][...] = turn_lanes(pre, cos_ref[...], sin_ref[...]).astype(BF16)


def attend_body(pad, pieces, blocks, query_ref, key_seg_ref, query_seg_ref, feature_ref, tok_ref,
                gains_ref, *refs):
    lse_ref, act_out, middle_out, second_out = refs[pieces + blocks :]
    row_count = query_ref.shape[0]
    allowed = allowed_pairs(key_seg_ref[...], query_seg_ref[...], row_count)
    joined = stacked(refs[pieces : pieces + blocks])
    queries = query_ref[...]
    outs = []
    for head in range(H):
        group = head // GROUP
        keys = joined[:, group * HD : (group + 1) * HD]
        values = joined[:, KVW + group * HD : KVW + (group + 1) * HD]
        head_query = queries[:, head * HD : (head + 1) * HD]
        scores = jnp.where(allowed, mm(keys, head_query, NT) * SCALE, MASKED_SCORE)
        largest = jnp.max(scores, axis=0, keepdims=True)
        weights = jnp.exp(scores - largest)
        total = jnp.sum(weights, axis=0, keepdims=True)
        lse_ref[head : head + 1, :] = largest + jnp.log(total)
        probs = (weights * (1.0 / total)).astype(BF16)
        outs.append(mm(probs, values, TN))
    attended = jnp.concatenate(outs, axis=1).astype(BF16)
    act = mm(attended, placed(feature_ref[...], attended.shape[1])).astype(BF16)
    act_out[...] = act
    middle = tok_ref[...].astype(F32) + mm(act, load_pair(refs[:pieces], 9 * pad, pad, 1))
    middle_out[...] = middle
    second_out[...] = (middle * inverse_norm(middle) * gains_ref[1:2, :]).astype(BF16)


def feed_body(hidden, pieces, at_ref, act_ref, other_ref, grad_ref, other_grad_ref, *refs):
    slot_rows = packed_rows(hidden)
    mine = load_packed(refs[:pieces], slot_rows, 0, hidden)
    copied = load_packed(refs[pieces : 2 * pieces], slot_rows, 0, hidden)
    down_weight = load_packed(refs[2 * pieces : 3 * pieces], slot_rows, 0, hidden)
    hidden_out, gate_out, up_out, own_out, send_out = refs[3 * pieces :]
    row_count = act_ref.shape[0]
    acts = jnp.concatenate([act_ref[...], other_ref[...]], axis=0)
    grads = jnp.concatenate([grad_ref[...], other_grad_ref[...]], axis=0)
    first = at_ref[2] == 0
    gate_weight = jnp.where(first, mine, copied)
    up_weight = jnp.where(first, copied, mine)
    gate = mm(acts, gate_weight, NT)
    up = mm(acts, up_weight, NT)
    back = mm(grads, down_weight, NT)
    sigmoid = jax.nn.sigmoid(gate)
    silu = gate * sigmoid
    hidden_out[...] = (silu * up).astype(BF16)
    gate_rows = (back * up * sigmoid * (1.0 + gate * (1.0 - sigmoid))).astype(BF16)
    up_rows = (back * silu).astype(BF16)
    gate_out[...] = gate_rows
    up_out[...] = up_rows
    second = mm(gate_rows, gate_weight) + mm(up_rows, up_weight)
    own_out[...] = second[:row_count]
    send_out[...] = second[row_count:].astype(BF16)


def feed_grads_body(hidden, kinds, *refs):
    lefts, right_refs = refs[:kinds], refs[kinds : kinds + 2]
    sent_out, kept_out = refs[kinds + 2 :]
    right = jnp.concatenate([right_refs[0][...], right_refs[1][...]], axis=0)
    half = lefts[0].shape[1] // 2
    for kind, left_ref in enumerate(lefts):
        left = left_ref[...]
        total = mm(left[:, half:], right, TN)
        for slot in range(half // hidden):
            store_packed(
                sent_out,
                (slot * kinds + kind) * packed_rows(hidden),
                total[slot * hidden : (slot + 1) * hidden],
            )
        total = mm(left[:, :half], right, TN)
        for slot in range(half // hidden):
            at = (slot * kinds + kind) * hidden
            kept_out[at : at + hidden, :] = total[slot * hidden : (slot + 1) * hidden]


def pair_grads_body(hidden, at_ref, gate_ref, up_ref, act_ref, other_ref, sent_out, kept_out):
    right = jnp.concatenate([act_ref[...], other_ref[...]], axis=0)
    gate = mm(gate_ref[...], right, TN)
    up = mm(up_ref[...], right, TN)
    first = at_ref[2] == 0
    kept_out[...] = jnp.where(first, gate, up)
    sent = jnp.where(first, up, gate)
    size = packed_rows(hidden)
    for slot in range(sent.shape[0] // hidden):
        store_packed(sent_out, slot * size, sent[slot * hidden : (slot + 1) * hidden])


def pair_sum_body(hidden, kept_ref, got_ref, sent_out, kept_out):
    size = packed_rows(hidden)
    total = kept_ref[...] + load_packed([got_ref], size, 0, hidden).astype(F32)
    half = total.shape[0] // 2
    kept_out[...] = total[:half]
    for slot in range(half // hidden):
        at = half + slot * hidden
        store_packed(sent_out, slot * size, total[at : at + hidden])


def result_body(hidden, hidden_ref, *refs):
    own_out, send_out = refs[-2:]
    row_count = own_out.shape[0]
    weights = load_packed(refs[:-2], packed_rows(hidden), 0, hidden)
    result = mm(hidden_ref[...], weights)
    own_out[...] = result[:row_count]
    send_out[...] = result[row_count:].astype(BF16)


def attend_back_body(pad, pieces, blocks, own_ref, got_ref, middle_ref, grad_ref, gains_ref, query_ref,
                     key_seg_ref, query_seg_ref, feature_ref, lse_ref, cos_ref, sin_ref, *refs):
    outs = refs[pieces + blocks :]
    query_out, rows_out, middle_grad_out, gain_out = outs[:4]
    block_outs = outs[4:]
    row_count = query_ref.shape[0]
    width = query_ref.shape[1]
    second_back = own_ref[...] + got_ref[...].astype(F32)
    middle = middle_ref[...]
    inverse = inverse_norm(middle)
    normed = middle * inverse
    gain_out[...] = jnp.broadcast_to(
        jnp.sum(second_back * normed, axis=0, keepdims=True), gain_out.shape
    )
    scaled = second_back * gains_ref[1:2, :]
    middle_grad = grad_ref[...].astype(F32) + inverse * (
        scaled - normed * jnp.mean(scaled * normed, axis=-1, keepdims=True)
    )
    middle_grad_out[...] = middle_grad
    attn_rows = middle_grad.astype(BF16)
    rows_out[...] = attn_rows
    by_slot = mm(attn_rows, load_pair(refs[:pieces], 9 * pad, pad, 1), NT).astype(BF16)
    rows = mm(by_slot, placed(feature_ref[...], width), NT).astype(BF16)

    allowed = allowed_pairs(key_seg_ref[...], query_seg_ref[...], row_count)
    joined = stacked(refs[pieces : pieces + blocks])
    queries = query_ref[...]
    query_parts, key_parts, value_parts = [], [], []
    for group in range(KVH):
        keys = joined[:, group * HD : (group + 1) * HD]
        values = joined[:, KVW + group * HD : KVW + (group + 1) * HD]
        key_sum, value_sum = None, None
        for head in range(group * GROUP, (group + 1) * GROUP):
            head_query = queries[:, head * HD : (head + 1) * HD]
            head_rows = rows[:, head * HD : (head + 1) * HD]
            scores = jnp.where(allowed, mm(keys, head_query, NT) * SCALE, MASKED_SCORE)
            exact = jnp.exp(scores - lse_ref[head : head + 1, :])
            dp = mm(values, head_rows, NT)
            weighted = exact * dp
            delta = jnp.sum(weighted, axis=0, keepdims=True)
            score_rows = (weighted - exact * delta).astype(BF16)
            query_parts.append(mm(score_rows, keys, TN) * SCALE)
            key_term = mm(score_rows, head_query)
            value_term = mm(exact.astype(BF16), head_rows)
            key_sum = key_term if key_sum is None else key_sum + key_term
            value_sum = value_term if value_sum is None else value_sum + value_term
        key_parts.append(key_sum * SCALE)
        value_parts.append(value_sum)
    joined_sum = jnp.concatenate(key_parts + value_parts, axis=1)
    for index, ref in enumerate(block_outs):
        ref[...] = joined_sum[index * row_count : (index + 1) * row_count].astype(ref.dtype)
    query_sum = jnp.concatenate(query_parts, axis=1)
    query_out[...] = turn_lanes(query_sum, cos_ref[...], -sin_ref[...]).astype(BF16)


def canonical(value, place):
    high = value.astype(BF16)
    low = (value - high.astype(F32)).astype(BF16)
    return mm(high, place, NT) + mm(low, place, NT)


def qo_grads_body(pad, act_ref, act_output_ref, query_ref, rows_ref, *refs):
    sent_out, query_kept, output_kept, back_out = refs[-4:]
    half = act_ref.shape[1] // 2
    lefts = ((act_ref[...], query_ref[...]), (act_output_ref[...], rows_ref[...]))
    sent = [mm(act[:, half:], rows, TN) for act, rows in lefts]
    for slot in range(half // pad):
        part = slice(slot * pad, (slot + 1) * pad)
        store_pair(sent_out, slot * 9 * pad, pad, sent[0][part], sent[1][part])
    for (act, rows), out in zip(lefts, (query_kept, output_kept)):
        out[...] = mm(act[:, :half], rows, TN)
    back_out[...] = mm(query_ref[...], load_pair(refs[:-4], 9 * pad, pad, 0), NT)


def kv_grads_body(shard, pad, pieces, blocks, act_ref, feature_ref, owner_ref, cos_ref, sin_ref,
                  back_ref, tok_ref, middle_grad_ref, gains_ref, second_gain_ref, *refs):
    weights = stacked(refs[:pieces])
    parts = refs[pieces : pieces + blocks]
    sent_out, kept_out, grad_out = refs[pieces + blocks :]
    width = tok_ref.shape[1]
    total = parts[0][...]
    for part in parts[1:]:
        total = total + part[...].astype(F32)
    turned = turn_lanes(total, cos_ref[...], -sin_ref[...])
    lane = lax.broadcasted_iota(jnp.int32, total.shape, 1)
    rows = jnp.where(lane < KVW, turned, total).astype(BF16)
    back = canonical(back_ref[...] + mm(rows, weights, NT), placed(feature_ref[...], width))
    source = tok_ref[...].astype(F32)
    inverse = inverse_norm(source)
    normed = source * inverse
    first_gain = jnp.sum(back * normed, axis=0, keepdims=True)
    slots = owner_ref.shape[0]
    spread = spread_lanes(shard, 2 * KVW, width)
    mine = owner_ref[...] == lax.broadcasted_iota(jnp.int32, (slots, width), 1) // shard
    place_at = lax.broadcasted_iota(jnp.int32, (slots, slots * pad), 1)
    slot_at = lax.broadcasted_iota(jnp.int32, (slots, slots * pad), 0)
    extra = None
    for index, gain in enumerate((first_gain, second_gain_ref[0:1, :])):
        by_slot = mm(jnp.where(mine, gain, 0.0).astype(BF16), spread, NT).astype(BF16)
        pick = jnp.where(place_at == slot_at * pad + shard + index, 1.0, 0.0).astype(BF16)
        term = mm(pick, by_slot, TN)
        extra = term if extra is None else extra + term
    grads = mm(act_ref[...], rows, TN) + extra
    half = grads.shape[0] // 2
    sent_out[...] = grads[half:].astype(BF16)
    kept_out[...] = grads[:half]
    scaled = back * gains_ref[0:1, :]
    input_grad = middle_grad_ref[...] + inverse * (
        scaled - normed * jnp.mean(scaled * normed, axis=-1, keepdims=True)
    )
    grad_out[...] = jnp.transpose(input_grad)


def core_sum_body(pad, query_ref, output_ref, qo_got, kv_ref, kv_got, sent_out, query_out,
                  output_out, kv_out):
    query = query_ref[...] + load_pair([qo_got], 9 * pad, pad, 0).astype(F32)
    output = output_ref[...] + load_pair([qo_got], 9 * pad, pad, 1).astype(F32)
    kv = kv_ref[...] + kv_got[...].astype(F32)
    half = query.shape[0] // 2
    query_out[...] = query[:half]
    output_out[...] = output[:half]
    kv_out[...] = kv[:half]
    for slot in range(half // pad):
        part = slice(half + slot * pad, half + (slot + 1) * pad)
        store_pair(sent_out, slot * 12 * pad, pad, query[part], output[part])
        store_three(sent_out, slot * 12 * pad + 9 * pad, pad, kv[part])


def x_sum_body(pad, query_ref, output_ref, kv_ref, got_ref, *outs):
    query = query_ref[...] + load_pair([got_ref], 12 * pad, pad, 0).astype(F32)
    output = output_ref[...] + load_pair([got_ref], 12 * pad, pad, 1).astype(F32)
    kv = kv_ref[...] + load_three([got_ref], 12 * pad, 9 * pad, pad).astype(F32)
    for slot, out in enumerate(outs):
        part = slice(slot * pad, (slot + 1) * pad)
        store_pair(out, 0, pad, query[part], output[part])
        store_three(out, 9 * pad, pad, kv[part])


def feed_sum_body(hidden, kinds, kept_ref, got_ref, *outs):
    size = packed_rows(hidden)
    for slot, out in enumerate(outs):
        for kind in range(kinds):
            at = slot * kinds + kind
            got = load_packed([got_ref.at[pl.ds(at * size, size), :]], size, 0, hidden)
            total = kept_ref[at * hidden : (at + 1) * hidden, :] + got.astype(F32)
            store_packed(out, kind * size, total)


def total_body(*refs):
    total = refs[0][...]
    for ref in refs[1:-1]:
        total = total + ref[...].astype(F32)
    refs[-1][...] = total.astype(BF16)


def copies_total(shard, pad, hidden, first, down_refs, feed_refs, rest_refs):
    size = packed_rows(hidden)
    down = two_copies_packed(down_refs, size, 0, hidden)
    own, got = [load_packed([ref], size, 0, hidden).astype(F32) for ref in feed_refs]
    gate, up = jnp.where(first, own, got), jnp.where(first, got, own)
    query = sum(load_pair([ref], 12 * pad, pad, 0).astype(F32) for ref in rest_refs)
    output = sum(load_pair([ref], 12 * pad, pad, 1).astype(F32) for ref in rest_refs)
    kv = sum(load_three([ref], 12 * pad, 9 * pad, pad).astype(F32) for ref in rest_refs)
    return (
        query[:shard],
        kv[:shard, :KVW],
        kv[:shard, KVW:],
        output[:shard],
        gate,
        up,
        down,
        kv[shard : shard + 2, :shard],
    )


def two_copies_packed(refs, slot_rows, base, rows):
    return sum(load_packed([ref], slot_rows, base, rows).astype(F32) for ref in refs)


def moment_messages_body(shard, pad, hidden, stride, at_ref, down_ref, down_got, feed_ref, feed_got,
                         rest_ref, rest_got, query_ref, key_ref, value_ref, output_ref, gate_ref,
                         up_ref, down_moment_ref, *refs):
    outs, scratch = refs[:-1], refs[-1]
    scratch[...] = jnp.zeros(scratch.shape, BF16)
    totals = copies_total(
        shard,
        pad,
        hidden,
        at_ref[2] == 0,
        (down_ref, down_got),
        (feed_ref, feed_got),
        (rest_ref, rest_got),
    )
    moments = [
        MOMENTUM * ref[...] + total
        for ref, total in zip(
            (query_ref, key_ref, value_ref, output_ref, gate_ref, up_ref, down_moment_ref), totals
        )
    ]
    for group, value in enumerate(moments[4:]):
        store_packed(scratch.at[group], 0, value)
    target = scratch.at[3]
    for which, value in enumerate((moments[0], moments[3])):
        for index in range(FULL):
            at = (which * FULL + index) * pad
            target[at : at + shard, :] = value[:, index * 128 : (index + 1) * 128].astype(BF16)
        at = 2 * FULL * pad
        target[at : at + shard, which * 64 : which * 64 + 64] = value[:, FULL * 128 :].astype(BF16)
    kv = jnp.concatenate([moments[1], moments[2]], axis=1)
    for index in range(3):
        at = (9 + index) * pad
        target[at : at + shard, :] = kv[:, index * 128 : (index + 1) * 128].astype(BF16)
    for other, out in enumerate(outs):
        out[...] = scratch[(at_ref[0] ^ other) // stride]


def moments_body(shard, pad, hidden, at_ref, down_ref, down_got, feed_ref, feed_got, rest_ref, rest_got,
                 middle_ref, result_ref, result_got, *refs):
    moments, grads, news, out_tokens = refs[:8], refs[8:16], refs[16:24], refs[24]
    totals = copies_total(
        shard,
        pad,
        hidden,
        at_ref[2] == 0,
        (down_ref, down_got),
        (feed_ref, feed_got),
        (rest_ref, rest_got),
    )
    for moment, total, grad, new in zip(moments, totals, grads, news):
        grad[...] = total
        new[...] = MOMENTUM * moment[...] + total
    result = middle_ref[...] + result_ref[...] + result_got[...].astype(F32)
    out_tokens[...] = jnp.transpose(result).astype(BF16)


def self_product(left, out_ref):
    size = left.shape[0]
    for start in range(0, size, 256):
        end = min(start + 256, size)
        block = mm(left[start:], left[start:end], NT)
        out_ref[start:, start:end] = block
        if end < size:
            out_ref[start:end, end:] = jnp.transpose(block[end - start :])


def polar_steps(wide_ref, gram_ref, needed):
    size = wide_ref.shape[0]
    first = wide_ref[...]
    norm = jnp.sqrt(jnp.sum(first * first)) + NORM_FLOOR
    wide_ref[...] = first / norm

    def step(columns):
        row = lax.broadcasted_iota(jnp.int32, (size, size), 0)
        col = lax.broadcasted_iota(jnp.int32, (size, size), 1)
        diagonal = row == col
        rounded = wide_ref[...].astype(BF16)
        self_product(rounded, gram_ref)
        gram = gram_ref[...]
        mean = jnp.sum(jnp.where(diagonal, gram, 0.0)) / size
        rest = gram - jnp.where(diagonal, mean, 0.0)
        self_product(rest.astype(BF16), gram_ref)
        square = gram_ref[...] + (2.0 * mean) * rest
        square = square + jnp.where(diagonal, mean * mean, 0.0)
        poly = CUBIC_TERM * gram + QUINTIC_TERM * square
        shift = jnp.sum(jnp.where(diagonal, poly, 0.0)) / size
        poly_rest = (poly - jnp.where(diagonal, shift, 0.0)).astype(BF16)
        wide_ref[:, :columns] = (LINEAR_TERM + shift) * wide_ref[:, :columns] + mm(
            poly_rest, rounded[:, :columns]
        )

    def middle_step(index, carry):
        step(wide_ref.shape[1])
        return carry

    lax.fori_loop(0, NS_STEPS - 1, middle_step, 0)
    step(needed)


def polar_body(pad, hidden, stride, slot_rows, pieces, at_ref, *refs):
    last = at_ref[0] // stride == 3

    @pl.when(last)
    def _():
        small_body(pad, slot_rows, pieces, at_ref, *refs)

    @pl.when(jnp.logical_not(last))
    def _():
        big_body(hidden, slot_rows, pieces, *refs)


def big_body(hidden, slot_rows, pieces, *refs):
    outs, wide_ref, gram_ref = refs[pieces:-4], refs[-4], refs[-2]
    tall = load_packed(refs[:pieces], slot_rows, 0, hidden)
    wide_ref[...] = jnp.transpose(tall.astype(F32))
    polar_steps(wide_ref, gram_ref, len(outs) * hidden)
    result = jnp.transpose(wide_ref[:, : len(outs) * hidden])
    for slot, out in enumerate(outs):
        if packed_rows(hidden) < out.shape[0]:
            out[...] = jnp.zeros(out.shape, BF16)
        store_packed(out, 0, result[slot * hidden : (slot + 1) * hidden])


def small_body(pad, slot_rows, pieces, at_ref, *refs):
    outs, large_ref, little_ref, gram_ref, little_gram_ref = refs[pieces:-4], *refs[-4:]
    ins = refs[:pieces]
    core = at_ref[1]
    large = jnp.where(
        core == 0,
        load_pair(ins, slot_rows, pad, 0).astype(F32),
        load_pair(ins, slot_rows, pad, 1).astype(F32),
    )
    little = load_three(ins, slot_rows, 9 * pad, pad).astype(F32)
    little = jnp.where(core == 0, little[:, :KVW], little[:, KVW : 2 * KVW])
    count = large.shape[0]
    large_ref[:, :count] = jnp.transpose(large)
    little_ref[...] = jnp.transpose(little)
    polar_steps(large_ref.at[:, :count], gram_ref, count)
    polar_steps(little_ref, little_gram_ref, count)
    large = jnp.transpose(large_ref[:, :count])
    little = jnp.transpose(little_ref[...])
    other = count // 2
    for slot, out in enumerate(outs):
        if 12 * pad < out.shape[0]:
            out[...] = jnp.zeros(out.shape, BF16)
        own = slice(slot * pad, (slot + 1) * pad)
        cross = slice(other + slot * pad, other + (slot + 1) * pad)
        store_pair(out, 0, pad, large[own], large[cross])
        store_three(
            out, 9 * pad, pad, jnp.concatenate([little[own], little[cross]], axis=1)
        )


def pick_body(stride, at_ref, *refs):
    answers, out = refs[:-1], refs[-1]
    for other, ref in enumerate(answers):

        @pl.when(at_ref[0] ^ other == 3 * stride)
        def _():
            out[...] = ref[...]


def weights_body(shard, pad, hidden, stride, factors, at_ref, *refs):
    count = len(refs) - 1 - 2 - 8 - 16
    answers = refs[:count]
    cross_ref, gain_moment_ref = refs[count : count + 2]
    masters = refs[count + 2 : count + 10]
    news, rounded = refs[count + 10 : count + 18], refs[count + 18 : count + 26]
    scratch = refs[-1]
    for group in range(4):
        for other, ref in enumerate(answers):

            @pl.when(at_ref[0] ^ other == group * stride)
            def _():
                scratch[group] = ref[...]

    core = at_ref[1]
    target = scratch.at[3]
    rows = target.shape[0]
    own_large = load_pair([target], rows, pad, 0)[:shard].astype(F32)
    other_large = load_pair([cross_ref], rows, pad, 1)[:shard].astype(F32)
    own_little = load_three([target], rows, 9 * pad, pad)[:shard, :KVW].astype(F32)
    other_little = load_three([cross_ref], rows, 9 * pad, pad)[:shard, KVW:].astype(F32)
    first = core == 0
    polars = (
        jnp.where(first, own_large, other_large),
        jnp.where(first, own_little, other_little),
        jnp.where(first, other_little, own_little),
        jnp.where(first, other_large, own_large),
    ) + tuple(
        load_packed([scratch.at[group]], rows, 0, hidden).astype(F32) for group in range(3)
    )
    for master, polar, factor, new, low in zip(masters, polars, factors, news, rounded):
        weight = master[...] - factor * polar
        new[...] = weight
        low[...] = weight.astype(BF16)
    weight = masters[7][...] - GAIN_RATE * gain_moment_ref[...]
    news[7][...] = weight
    rounded[7][...] = weight.astype(BF16)


def local(
    tokens,
    out_grad,
    segments,
    query_copy,
    key_copy,
    value_copy,
    output_copy,
    gate_copy,
    up_copy,
    down_copy,
    gains_copy,
    query_master,
    key_master,
    value_master,
    output_master,
    gate_master,
    up_master,
    down_master,
    gains_master,
    query_moment,
    key_moment,
    value_moment,
    output_moment,
    gate_moment,
    up_moment,
    down_moment,
    gains_moment,
):
    x_size, z_size = lax.axis_size("x"), lax.axis_size("ctx")
    x_at, core_at, z_at = lax.axis_index("x"), lax.axis_index("core"), lax.axis_index("ctx")
    if z_size % 4:
        raise ValueError("ctx size")
    stride = z_size // 4
    slots = 2 * x_size * z_size
    rows, width = tokens.shape[1], tokens.shape[2]
    shard = query_copy.shape[0]
    pad = -(-(shard + 2) // 8) * 8
    hidden = down_copy.shape[0]
    back_blocks = z_size // 2
    blocks = back_blocks + 1
    at = jnp.stack([z_at, core_at, lax.axis_index("rep"), x_at]).astype(jnp.int32)
    bind = functools.partial

    def join(parts):
        total = sum(part.shape[0] for part in parts)
        return call(join_body, shaped(parts[0].dtype, total, parts[0].shape[1]), *parts)

    def along_ctx(value, packed=False):
        parts = [value] + [flip(value, "ctx", other) for other in range(1, z_size)]
        if packed:
            out = shaped(BF16, z_size * packed_rows(value.shape[0]), 128)
            return call(pack_body, out, *parts)
        return join(parts)

    def along_x(pieces):
        for bit in bits_of(x_size):
            pieces = pieces + [flip(piece, "x", bit) for piece in pieces]
        return pieces

    def along_core(pieces):
        return pieces + [flip(piece, "core", 1) for piece in pieces]

    kv_message = call(
        bind(kv_message_body, shard), shaped(BF16, pad, 2 * KVW), key_copy, value_copy, gains_copy,
    )
    kv_joined = along_ctx(kv_message)
    frequency = np.float32(ROPE_BASE) ** (
        np.float32(-2.0) * (np.arange(128) % (HD // 2)).astype(np.float32) / np.float32(HD)
    )
    tok, grad, cosine, sine, key_seg, query_seg, feature, owner = call(
        bind(setup_body, blocks, shard, pad, x_size, z_size),
        (
            shaped(BF16, rows, width),
            shaped(BF16, rows, width),
            shaped(F32, rows, 128),
            shaped(F32, rows, 128),
            shaped(F32, blocks * rows, 1),
            shaped(F32, 1, rows),
            shaped(jnp.int32, 1, slots * pad),
            shaped(jnp.int32, slots, 1),
        ),
        at,
        tokens[0].T,
        out_grad[0].T,
        segments,
        jnp.asarray(frequency[None, :], F32),
        scalars=1,
    )
    qo_message = call(
        bind(qo_message_body, shard, pad), shaped(BF16, 9 * pad, 128), query_copy, output_copy
    )
    size = packed_rows(hidden)
    feed_shard = jnp.where(lax.axis_index("rep") == 0, gate_copy.T, up_copy.T)
    kv_pieces = along_core(along_x([kv_joined]))
    qo_pieces = along_core(along_x([along_ctx(qo_message)]))
    other_grad = flip(grad, "core", 1)
    pieces = len(kv_pieces)

    kv_own, _, act_slots, gains = call(
        bind(kv_body, shard, pad, pieces),
        (
            shaped(BF16, rows, 2 * KVW),
            shaped(BF16, rows, width),
            shaped(BF16, rows, slots * pad),
            shaped(F32, 8, width),
        ),
        tok,
        feature,
        owner,
        cosine,
        sine,
        *kv_pieces,
    )
    kv_blocks = [kv_own]
    following = [(i, i + 1) for i in range(z_size - 1)]
    for _ in range(1, blocks):
        kv_blocks.append(lax.ppermute(kv_blocks[-1], "ctx", following))
    mine_pieces = along_x([along_ctx(feed_shard, True)])
    copied_pieces = [flip(piece, "rep", 1) for piece in mine_pieces]
    down_pieces = along_x([along_ctx(down_copy, True)])
    feed_pieces = len(down_pieces)
    queries = call(
        bind(query_body, pad), shaped(BF16, rows, width), act_slots, cosine, sine, *qo_pieces,
    )
    lse, act_output, middle, act_second = call(
        bind(attend_body, pad, pieces, blocks),
        (
            shaped(F32, H, rows),
            shaped(BF16, rows, slots * pad),
            shaped(F32, rows, width),
            shaped(BF16, rows, width),
        ),
        queries,
        key_seg,
        query_seg,
        feature,
        tok,
        gains,
        *qo_pieces,
        *kv_blocks,
    )

    other_act = flip(act_second, "core", 1)
    inner = slots // 2 * hidden
    hidden_rows, gate_rows, up_rows, second_own, second_send = call(
        bind(feed_body, hidden, feed_pieces),
        (shaped(BF16, 2 * rows, inner),) * 3
        + (shaped(F32, rows, width), shaped(BF16, rows, width)),
        at,
        act_second,
        other_act,
        grad,
        other_grad,
        *mine_pieces,
        *copied_pieces,
        *down_pieces,
        scalars=1,
    )
    second_got = flip(second_send, "core", 1)
    kept_slots = slots // 4

    def feed_gradients(lefts, rights):
        kinds = len(lefts)
        sent, kept = call(
            bind(feed_grads_body, hidden, kinds),
            (
                shaped(BF16, kept_slots * kinds * size, 128),
                shaped(F32, kept_slots * kinds * hidden, width),
            ),
            *lefts,
            *rights,
        )
        return sent, kept, flip(sent, "x", 1)

    def feed_totals(kinds, kept, got):
        parts = call(
            bind(feed_sum_body, hidden, kinds),
            (shaped(F32, kinds * size, 128),)
            + (shaped(BF16, kinds * size, 128),) * (z_size - 1),
            kept,
            got,
        )
        return [parts[0]] + [flip(parts[other], "ctx", other) for other in range(1, z_size)]

    def added(parts):
        total = call(total_body, shaped(BF16, *parts[0].shape), *parts)
        return total, flip(total, "rep", 1)

    _, down_kept, down_got = feed_gradients([hidden_rows], [grad, other_grad])
    pair_sent, pair_kept = call(
        bind(pair_grads_body, hidden),
        (shaped(BF16, slots // 2 * size, 128), shaped(F32, slots // 2 * hidden, width)),
        at,
        gate_rows,
        up_rows,
        act_second,
        other_act,
        scalars=1,
    )
    pair_got = flip(pair_sent, "rep", 1)
    feed_sent, feed_kept = call(
        bind(pair_sum_body, hidden),
        (shaped(BF16, kept_slots * size, 128), shaped(F32, kept_slots * hidden, width)),
        pair_kept,
        pair_got,
    )
    feed_got = flip(feed_sent, "x", 1)

    outs = call(
        bind(attend_back_body, pad, pieces, blocks),
        (
            shaped(BF16, rows, width),
            shaped(BF16, rows, width),
            shaped(F32, rows, width),
            shaped(F32, 8, width),
            shaped(F32, rows, 2 * KVW),
        )
        + (shaped(BF16, rows, 2 * KVW),) * back_blocks,
        second_own,
        second_got,
        middle,
        grad,
        gains,
        queries,
        key_seg,
        query_seg,
        feature,
        lse,
        cosine,
        sine,
        *qo_pieces,
        *kv_blocks,
    )
    query_rows, attn_rows, middle_grad, second_gain = outs[:4]
    kv_terms = [outs[4]]
    for back in range(1, blocks):
        pairs = [(i + back, i) for i in range(z_size - back)]
        kv_terms.append(lax.ppermute(outs[4 + back], "ctx", pairs))
    down_parts = feed_totals(1, down_kept, down_got)

    qo_sent, query_kept, output_kept, query_back = call(
        bind(qo_grads_body, pad),
        (
            shaped(BF16, slots // 2 * 9 * pad, 128),
            shaped(F32, slots // 2 * pad, width),
            shaped(F32, slots // 2 * pad, width),
            shaped(F32, rows, slots * pad),
        ),
        act_slots,
        act_output,
        query_rows,
        attn_rows,
        *qo_pieces,
    )
    qo_got = flip(qo_sent, "core", 1)
    kv_sent, kv_kept, input_grad = call(
        bind(kv_grads_body, shard, pad, pieces, blocks),
        (
            shaped(BF16, slots // 2 * pad, 2 * KVW),
            shaped(F32, slots // 2 * pad, 2 * KVW),
            shaped(F32, width, rows),
        ),
        act_slots,
        feature,
        owner,
        cosine,
        sine,
        query_back,
        tok,
        middle_grad,
        gains,
        second_gain,
        *kv_pieces,
        *kv_terms,
    )
    kv_got = flip(kv_sent, "core", 1)
    feed_parts = feed_totals(1, feed_kept, feed_got)
    rest_sent, query_kept, output_kept, kv_kept = call(
        bind(core_sum_body, pad),
        (
            shaped(BF16, kept_slots * 12 * pad, 128),
            shaped(F32, kept_slots * pad, width),
            shaped(F32, kept_slots * pad, width),
            shaped(F32, kept_slots * pad, 2 * KVW),
        ),
        query_kept,
        output_kept,
        qo_got,
        kv_kept,
        kv_got,
    )
    rest_got = flip(rest_sent, "x", 1)
    down_total, down_copied = added(down_parts)
    result_own, result_send = call(
        bind(result_body, hidden),
        (shaped(F32, rows, width), shaped(BF16, rows, width)),
        hidden_rows,
        *down_pieces,
    )
    result_got = flip(result_send, "core", 1)
    rest_parts = call(
        bind(x_sum_body, pad),
        (shaped(F32, 12 * pad, 128),) + (shaped(BF16, 12 * pad, 128),) * (z_size - 1),
        query_kept,
        output_kept,
        kv_kept,
        rest_got,
    )
    rest_parts = [rest_parts[0]] + [
        flip(rest_parts[other], "ctx", other) for other in range(1, z_size)
    ]
    feed_total, feed_copied = added(feed_parts)
    rest_total, rest_copied = added(rest_parts)

    slot_rows = max(size, 12 * pad)
    message = shaped(BF16, slot_rows, 128)
    sums = (down_total, down_copied, feed_total, feed_copied, rest_total, rest_copied)
    natural = (
        query_moment,
        key_moment,
        value_moment,
        output_moment,
        gate_moment.T,
        up_moment.T,
        down_moment,
        gains_moment,
    )
    messages = call(
        bind(moment_messages_body, shard, pad, hidden, stride),
        (message,) * z_size,
        at,
        *sums,
        *natural[:7],
        scratch=[pltpu.VMEM((4, slot_rows, 128), BF16)],
        scalars=1,
    )
    owner_columns = [g * stride for g in range(4)]
    arrived = [messages[0]]
    for other in range(1, z_size):
        pairs = [(d ^ other, d) for d in owner_columns]
        arrived.append(lax.ppermute(messages[other], "ctx", pairs))
    matrix_pieces = along_core(along_x([join(arrived)]))
    moment_types = tuple(shaped(F32, *value.shape) for value in natural)
    outs = call(
        bind(moments_body, shard, pad, hidden),
        moment_types * 2 + (shaped(BF16, width, rows),),
        at,
        *sums,
        middle,
        result_own,
        result_got,
        *natural,
        scalars=1,
    )
    totals, new_moments, out_tokens = list(outs[:8]), list(outs[8:16]), outs[16]

    large_lanes = max(hidden, pad) * slots

    solved = call(
        bind(polar_body, pad, hidden, stride, slot_rows, pieces),
        (message,) * z_size,
        at,
        *matrix_pieces,
        scratch=[
            pltpu.VMEM((width, large_lanes), F32),
            pltpu.VMEM((KVW, slots * pad), F32),
            pltpu.VMEM((width, width), F32),
            pltpu.VMEM((KVW, KVW), F32),
        ],
        scalars=1,
    )
    answers = [solved[0]]
    for other in range(1, z_size):
        pairs = [(d, d ^ other) for d in owner_columns]
        answers.append(lax.ppermute(solved[other], "ctx", pairs))
    picked = call(bind(pick_body, stride), message, at, *answers, scalars=1)
    crossed = flip(picked, "core", 1)
    masters = (
        query_master,
        key_master,
        value_master,
        output_master,
        gate_master.T,
        up_master.T,
        down_master,
        gains_master,
    )
    full = slots * hidden
    full_shapes = (
        (width, width),
        (width, KVW),
        (width, KVW),
        (width, width),
        (width, full),
        (width, full),
        (full, width),
    )
    factors = [STEP_SIZE * math.sqrt(max(shape) / shape[0]) for shape in full_shapes]
    outs = call(
        bind(weights_body, shard, pad, hidden, stride, factors),
        tuple(shaped(F32, *value.shape) for value in masters)
        + tuple(shaped(BF16, *value.shape) for value in masters),
        at,
        *answers,
        crossed,
        new_moments[7],
        *masters,
        scratch=[pltpu.VMEM((4, slot_rows, 128), BF16)],
        scalars=1,
    )
    weights, rounded = list(outs[:8]), list(outs[8:])
    for values in (totals, new_moments, weights, rounded):
        for index in (4, 5):
            values[index] = values[index].T
    return (out_tokens.T[None], input_grad.T[None], *totals, *new_moments, *weights, *rounded)


def solution(mesh):
    dp_size, ctx_size, rep_size = (mesh.shape[name] for name in ("dp", "ctx", "rep"))
    split = Mesh(
        mesh.devices.reshape(dp_size // 2, 2, ctx_size, rep_size), ("x", "core", "ctx", "rep")
    )
    batch = ("x", "core", "rep")
    parts = ("x", "core", "ctx")
    by_row, by_column = P(parts, None), P(None, parts)
    weights = (by_row, by_row, by_row, by_row, by_column, by_column, by_row, by_column)
    token_spec = P(batch, "ctx", None)

    return jax.shard_map(
        local,
        mesh=split,
        in_specs=(token_spec, token_spec, P(batch, None)) + weights * 3,
        out_specs=(token_spec, token_spec) + weights * 4,
        check_vma=False,
    )
```

```python
import functools
import math

import jax
import jax.numpy as jnp
import numpy as np
from jax import lax
from jax.experimental import pallas as pl
from jax.experimental.pallas import tpu as pltpu
from jax.sharding import Mesh
from jax.sharding import PartitionSpec as P


H = 9
KVH = 3
HD = 64
GROUP = H // KVH
KVW = KVH * HD
NS_STEPS = 5

EPSILON = 1e-05
ROPE_BASE = 10000.0
MASKED_SCORE = -1e30
MOMENTUM = 0.5
STEP_SIZE = 0.5
GAIN_RATE = 0.001
LINEAR_TERM = 3.4445
CUBIC_TERM = -4.775
QUINTIC_TERM = 2.0315
NORM_FLOOR = 1e-07
SCALE = HD ** (-0.5)

F32 = jnp.float32
BF16 = jnp.bfloat16


NN = (((1,), (0,)), ((), ()))
NT = (((1,), (1,)), ((), ()))
TN = (((0,), (0,)), ((), ()))


def mm(left, right, dims=NN):
    return lax.dot_general(left, right, dims, preferred_element_type=F32)


def flip(value, axis, bit):
    return lax.ppermute(value, axis, [(i, i ^ bit) for i in range(lax.axis_size(axis))])


def bits_of(size):
    bits = []
    while size > 1:
        size //= 2
        bits.append(size)
    return bits


def call(body, out_shape, *operands, scratch=(), scalars=0):
    specs = [pl.BlockSpec(memory_space=pltpu.SMEM)] * scalars
    specs += [pl.BlockSpec(memory_space=pltpu.VMEM)] * (len(operands) - scalars)
    return pl.pallas_call(
        body,
        out_shape=out_shape,
        in_specs=specs,
        scratch_shapes=scratch,
        compiler_params=pltpu.CompilerParams(vmem_limit_bytes=56 * 1024 * 1024),
    )(*operands)


def shaped(dtype, *shape):
    return jax.ShapeDtypeStruct(shape, dtype)


def turn_chunk(chunk, cosine, sine):
    lane = lax.broadcasted_iota(jnp.int32, chunk.shape, 1)
    turned = jnp.where(
        lane % HD < HD // 2,
        pltpu.roll(chunk, 128 - HD // 2, 1),
        pltpu.roll(chunk, HD // 2, 1),
    )
    return chunk * cosine + turned * sine


def turn_lanes(full, cosine, sine):
    width = full.shape[1]
    pieces = []
    for start in range(0, width - width % 128, 128):
        pieces.append(turn_chunk(full[:, start : start + 128], cosine, sine))
    if width % 128:
        last = full[:, width - 64 :]
        pieces.append(turn_chunk(jnp.concatenate([last, last], axis=1), cosine, sine)[:, :64])
    return jnp.concatenate(pieces, axis=1)


def allowed_pairs(key_seg, query_seg, row_count):
    shape = (key_seg.shape[0], query_seg.shape[1])
    key_row = lax.broadcasted_iota(jnp.int32, shape, 0)
    query_col = lax.broadcasted_iota(jnp.int32, shape, 1)
    earlier = (key_row >= row_count) | (key_row <= query_col)
    return (key_seg == query_seg) & earlier


def placed(feature, width):
    at = lax.broadcasted_iota(jnp.int32, (width, feature.shape[1]), 0)
    return jnp.where(at == feature, 1.0, 0.0).astype(BF16)


def stacked(refs):
    return jnp.concatenate([ref[...] for ref in refs], axis=0)


def inverse_norm(value):
    return lax.rsqrt(jnp.mean(value * value, axis=-1, keepdims=True) + EPSILON)


FULL = 4


def cut(rows):
    return min(rows, -(-((rows + 1) // 2) // 16) * 16)


def packed_rows(rows):
    return FULL * rows + cut(rows)


def store_packed(out, base, value):
    rows, dtype = value.shape[0], out.dtype
    low = cut(rows)
    for index in range(FULL):
        at = base + index * rows
        out[at : at + rows, :] = value[:, index * 128 : (index + 1) * 128].astype(dtype)
    at = base + FULL * rows
    out[at : at + low, 0:64] = value[:low, FULL * 128 :].astype(dtype)
    if rows - low < low:
        out[at : at + low, 64:128] = jnp.zeros((low, 64), dtype)
    if rows > low:
        out[at : at + rows - low, 64:128] = value[low:, FULL * 128 :].astype(dtype)


def load_packed(refs, slot_rows, base, rows):
    places = [(ref, at + base) for ref in refs for at in range(0, ref.shape[0], slot_rows)]
    low = cut(rows)
    columns = []
    for index in range(FULL):
        columns.append(
            jnp.concatenate(
                [ref[at + index * rows : at + (index + 1) * rows, :] for ref, at in places], axis=0
            )
        )
    rest = []
    for ref, at in places:
        first = at + FULL * rows
        rest.append(ref[first : first + low, 0:64])
        if rows > low:
            rest.append(ref[first : first + rows - low, 64:128])
    columns.append(jnp.concatenate(rest, axis=0))
    return jnp.concatenate(columns, axis=1)


def store_pair(out, base, pad, first, second):
    for which, value in enumerate((first, second)):
        for index in range(FULL):
            at = base + (which * FULL + index) * pad
            out[at : at + pad, :] = value[:, index * 128 : (index + 1) * 128].astype(out.dtype)
        at = base + 2 * FULL * pad
        out[at : at + pad, which * 64 : which * 64 + 64] = value[:, FULL * 128 :].astype(out.dtype)


def load_pair(refs, slot_rows, pad, which):
    places = [(ref, at) for ref in refs for at in range(0, ref.shape[0], slot_rows)]
    columns = []
    for index in range(FULL):
        first = (which * FULL + index) * pad
        columns.append(
            jnp.concatenate([ref[at + first : at + first + pad, :] for ref, at in places], axis=0)
        )
    first = 2 * FULL * pad
    columns.append(
        jnp.concatenate(
            [
                ref[at + first : at + first + pad, which * 64 : which * 64 + 64]
                for ref, at in places
            ],
            axis=0,
        )
    )
    return jnp.concatenate(columns, axis=1)


def store_three(out, base, pad, value):
    for index in range(3):
        at = base + index * pad
        out[at : at + pad, :] = value[:, index * 128 : (index + 1) * 128].astype(out.dtype)


def load_three(refs, slot_rows, base, pad):
    places = [(ref, at + base) for ref in refs for at in range(0, ref.shape[0], slot_rows)]
    columns = [
        jnp.concatenate(
            [ref[at + index * pad : at + (index + 1) * pad, :] for ref, at in places], axis=0
        )
        for index in range(3)
    ]
    return jnp.concatenate(columns, axis=1)


def kv_message_body(shard, key_ref, value_ref, gains_ref, out_ref):
    out_ref[...] = jnp.zeros(out_ref.shape, BF16)
    out_ref[0:shard, 0:KVW] = key_ref[...]
    out_ref[0:shard, KVW : 2 * KVW] = value_ref[...]
    out_ref[shard : shard + 2, 0:shard] = gains_ref[...]


def qo_message_body(shard, pad, query_ref, output_ref, out_ref):
    out_ref[...] = jnp.zeros(out_ref.shape, BF16)
    for which, ref in enumerate((query_ref, output_ref)):
        for index in range(FULL):
            at = (which * FULL + index) * pad
            out_ref[at : at + shard, :] = ref[:, index * 128 : (index + 1) * 128]
        at = 2 * FULL * pad
        out_ref[at : at + shard, which * 64 : which * 64 + 64] = ref[:, FULL * 128 :]


def shard_of(position, at_ref, x_size, z_size):
    z_part = at_ref[0] ^ (position & (z_size - 1))
    x_part = at_ref[3] ^ ((position // z_size) & (x_size - 1))
    core_part = at_ref[1] ^ (position // (z_size * x_size))
    return (x_part * 2 + core_part) * z_size + z_part


def setup_body(blocks, shard, pad, x_size, z_size, at_ref, tok_ref, grad_ref, seg_ref,
               frequency_ref, tok_out, grad_out, cos_out, sin_out, key_seg_out, query_seg_out,
               feature_out, owner_out):
    rows = tok_ref.shape[1]
    tok_out[...] = jnp.transpose(tok_ref[...])
    grad_out[...] = jnp.transpose(grad_ref[...])
    z_at = at_ref[0]
    every = [seg_ref[:, block * rows : (block + 1) * rows].astype(F32) for block in range(z_size)]

    def row_of(wanted):
        row = jnp.full((1, rows), -1.0, F32)
        for block, value in enumerate(every):
            row = jnp.where(wanted == block, value, row)
        return row

    def upright(row):
        return jnp.transpose(jnp.broadcast_to(row, (8, rows)))[:, 0:1]

    own = row_of(z_at)
    own_column = upright(own)
    query_seg_out[...] = own
    key_seg_out[0:rows, :] = own_column
    for back in range(1, blocks):
        key_seg_out[back * rows : (back + 1) * rows, :] = upright(row_of(z_at - back))
    first = jnp.zeros((rows, 1), F32)
    for value in every:
        first = first + jnp.sum(jnp.where(value < own_column, 1.0, 0.0), axis=1, keepdims=True)
    index = lax.broadcasted_iota(jnp.int32, (rows, 1), 0) + z_at * rows
    angles = (index.astype(F32) - first) * frequency_ref[...]
    lane = lax.broadcasted_iota(jnp.int32, angles.shape, 1)
    cos_out[...] = jnp.cos(angles)
    sin_out[...] = jnp.sin(angles) * jnp.where(lane % HD < HD // 2, -1.0, 1.0)
    column = lax.broadcasted_iota(jnp.int32, feature_out.shape, 1)
    slot = jnp.floor((column.astype(F32) + 0.5) / pad).astype(jnp.int32)
    inside = column - slot * pad
    feature = shard_of(slot, at_ref, x_size, z_size) * shard + inside
    feature_out[...] = jnp.where(inside < shard, feature, -1)
    position = lax.broadcasted_iota(jnp.int32, owner_out.shape, 0)
    owner_out[...] = shard_of(position, at_ref, x_size, z_size)


def join_body(*refs):
    out, at = refs[-1], 0
    for ref in refs[:-1]:
        out[at : at + ref.shape[0], :] = ref[...]
        at += ref.shape[0]


def pack_body(*refs):
    out = refs[-1]
    size = packed_rows(refs[0].shape[0])
    for slot, ref in enumerate(refs[:-1]):
        store_packed(out, slot * size, ref[...])


def kv_body(shard, pad, pieces, tok_ref, feature_ref, owner_ref, cos_ref, sin_ref, *refs):
    kv_out, act_out, act_kv_out, gains_out = refs[pieces:]
    weights = stacked(refs[:pieces])
    source = tok_ref[...].astype(F32)
    width = source.shape[1]
    slots = owner_ref.shape[0]
    place_at = lax.broadcasted_iota(jnp.int32, (slots, slots * pad), 1)
    slot_at = lax.broadcasted_iota(jnp.int32, (slots, slots * pad), 0)
    spread = spread_lanes(shard, 2 * KVW, width)
    mine = owner_ref[...] == lax.broadcasted_iota(jnp.int32, (slots, width), 1) // shard
    gains_out[...] = jnp.zeros(gains_out.shape, F32)
    for index in range(2):
        pick = jnp.where(place_at == slot_at * pad + shard + index, 1.0, 0.0).astype(BF16)
        by_slot = mm(pick, weights).astype(BF16)
        gain = jnp.sum(jnp.where(mine, mm(by_slot, spread), 0.0), axis=0, keepdims=True)
        gains_out[index : index + 1, :] = gain
    act = (source * inverse_norm(source) * gains_out[0:1, :]).astype(BF16)
    act_out[...] = act
    act_kv = mm(act, placed(feature_ref[...], width)).astype(BF16)
    act_kv_out[...] = act_kv
    pre = mm(act_kv, weights)
    turned = turn_lanes(pre, cos_ref[...], sin_ref[...])
    lane = lax.broadcasted_iota(jnp.int32, pre.shape, 1)
    kv_out[...] = jnp.where(lane < KVW, turned, pre).astype(BF16)


def spread_lanes(shard, lanes, width):
    lane = lax.broadcasted_iota(jnp.int32, (lanes, width), 0)
    feature = lax.broadcasted_iota(jnp.int32, (lanes, width), 1)
    return jnp.where((feature % shard == lane) & (lane < shard), 1.0, 0.0).astype(BF16)


def query_body(pad, act_ref, cos_ref, sin_ref, *refs):
    weights = load_pair(refs[:-1], 9 * pad, pad, 0)
    pre = mm(act_ref[...], weights)
    refs[-1][...] = turn_lanes(pre, cos_ref[...], sin_ref[...]).astype(BF16)


def spread_heads(value, ref, first=0):
    for index in range(ref.shape[0]):
        at = (first + index) * HD
        ref[index] = value[:, at : at + HD]


def gathered_heads(ref):
    return jnp.concatenate([ref[index] for index in range(ref.shape[0])], axis=1)


def attend_body(pad, pieces, blocks, query_ref, key_seg_ref, query_seg_ref, feature_ref, tok_ref,
                gains_ref, *refs):
    lse_ref, act_out, middle_out, second_out = refs[pieces + blocks : -4]
    query_heads, key_heads, value_heads, out_heads = refs[-4:]
    row_count = query_ref.shape[0]
    allowed = allowed_pairs(key_seg_ref[...], query_seg_ref[...], row_count)
    joined = stacked(refs[pieces : pieces + blocks])
    spread_heads(query_ref[...], query_heads)
    spread_heads(joined, key_heads)
    spread_heads(joined, value_heads, KVH)

    def one_group(group):
        keys, values = key_heads[group], value_heads[group]
        for member in range(GROUP):
            head = group * GROUP + member
            scores = jnp.where(allowed, mm(keys, query_heads[head], NT) * SCALE, MASKED_SCORE)
            largest = jnp.max(scores, axis=0, keepdims=True)
            weights = jnp.exp(scores - largest)
            total = jnp.sum(weights, axis=0, keepdims=True)
            lse_ref[head] = largest + jnp.log(total)
            probs = (weights * (1.0 / total)).astype(BF16)
            out_heads[head] = mm(probs, values, TN).astype(BF16)

    for group in range(KVH):
        one_group(group)
    attended = gathered_heads(out_heads)
    act = mm(attended, placed(feature_ref[...], attended.shape[1])).astype(BF16)
    act_out[...] = act
    middle = tok_ref[...].astype(F32) + mm(act, load_pair(refs[:pieces], 9 * pad, pad, 1))
    middle_out[...] = middle
    second_out[...] = (middle * inverse_norm(middle) * gains_ref[1:2, :]).astype(BF16)


def feed_body(hidden, pieces, at_ref, act_ref, other_ref, grad_ref, other_grad_ref, *refs):
    slot_rows = packed_rows(hidden)
    mine = load_packed(refs[:pieces], slot_rows, 0, hidden)
    copied = load_packed(refs[pieces : 2 * pieces], slot_rows, 0, hidden)
    down_weight = load_packed(refs[2 * pieces : 3 * pieces], slot_rows, 0, hidden)
    hidden_out, gate_out, up_out, own_out, send_out = refs[3 * pieces :]
    row_count = act_ref.shape[0]
    acts = jnp.concatenate([act_ref[...], other_ref[...]], axis=0)
    grads = jnp.concatenate([grad_ref[...], other_grad_ref[...]], axis=0)
    first = at_ref[2] == 0
    gate_weight = jnp.where(first, mine, copied)
    up_weight = jnp.where(first, copied, mine)
    gate = mm(acts, gate_weight, NT)
    up = mm(acts, up_weight, NT)
    back = mm(grads, down_weight, NT)
    sigmoid = jax.nn.sigmoid(gate)
    silu = gate * sigmoid
    hidden_out[...] = (silu * up).astype(BF16)
    gate_rows = (back * up * sigmoid * (1.0 + gate * (1.0 - sigmoid))).astype(BF16)
    up_rows = (back * silu).astype(BF16)
    gate_out[...] = gate_rows
    up_out[...] = up_rows
    second = mm(gate_rows, gate_weight) + mm(up_rows, up_weight)
    own_out[...] = second[:row_count]
    send_out[...] = second[row_count:].astype(BF16)


def feed_grads_body(hidden, kinds, *refs):
    lefts, right_refs = refs[:kinds], refs[kinds : kinds + 2]
    sent_out, kept_out = refs[kinds + 2 :]
    right = jnp.concatenate([right_refs[0][...], right_refs[1][...]], axis=0)
    half = lefts[0].shape[1] // 2
    for kind, left_ref in enumerate(lefts):
        left = left_ref[...]
        total = mm(left[:, half:], right, TN)
        for slot in range(half // hidden):
            store_packed(
                sent_out,
                (slot * kinds + kind) * packed_rows(hidden),
                total[slot * hidden : (slot + 1) * hidden],
            )
        total = mm(left[:, :half], right, TN)
        for slot in range(half // hidden):
            at = (slot * kinds + kind) * hidden
            kept_out[at : at + hidden, :] = total[slot * hidden : (slot + 1) * hidden]


def pair_grads_body(hidden, at_ref, gate_ref, up_ref, act_ref, other_ref, sent_out, kept_out):
    right = jnp.concatenate([act_ref[...], other_ref[...]], axis=0)
    gate = mm(gate_ref[...], right, TN)
    up = mm(up_ref[...], right, TN)
    first = at_ref[2] == 0
    kept_out[...] = jnp.where(first, gate, up)
    sent = jnp.where(first, up, gate)
    size = packed_rows(hidden)
    for slot in range(sent.shape[0] // hidden):
        store_packed(sent_out, slot * size, sent[slot * hidden : (slot + 1) * hidden])


def pair_sum_body(hidden, kept_ref, got_ref, sent_out, kept_out):
    size = packed_rows(hidden)
    total = kept_ref[...] + load_packed([got_ref], size, 0, hidden).astype(F32)
    half = total.shape[0] // 2
    kept_out[...] = total[:half]
    for slot in range(half // hidden):
        at = half + slot * hidden
        store_packed(sent_out, slot * size, total[at : at + hidden])


def result_body(hidden, hidden_ref, *refs):
    own_out, send_out = refs[-2:]
    row_count = own_out.shape[0]
    weights = load_packed(refs[:-2], packed_rows(hidden), 0, hidden)
    result = mm(hidden_ref[...], weights)
    own_out[...] = result[:row_count]
    send_out[...] = result[row_count:].astype(BF16)


def attend_back_body(pad, pieces, blocks, own_ref, got_ref, middle_ref, grad_ref, gains_ref, query_ref,
                     key_seg_ref, query_seg_ref, feature_ref, lse_ref, cos_ref, sin_ref, *refs):
    outs = refs[pieces + blocks : -7]
    query_heads, row_heads, key_heads, value_heads = refs[-7:-3]
    query_sums, key_sums, value_sums = refs[-3:]
    query_out, rows_out, middle_grad_out, gain_out = outs[:4]
    block_outs = outs[4:]
    row_count = query_ref.shape[0]
    width = query_ref.shape[1]
    second_back = own_ref[...] + got_ref[...].astype(F32)
    middle = middle_ref[...]
    inverse = inverse_norm(middle)
    normed = middle * inverse
    gain_out[...] = jnp.broadcast_to(
        jnp.sum(second_back * normed, axis=0, keepdims=True), gain_out.shape
    )
    scaled = second_back * gains_ref[1:2, :]
    middle_grad = grad_ref[...].astype(F32) + inverse * (
        scaled - normed * jnp.mean(scaled * normed, axis=-1, keepdims=True)
    )
    middle_grad_out[...] = middle_grad
    attn_rows = middle_grad.astype(BF16)
    rows_out[...] = attn_rows
    by_slot = mm(attn_rows, load_pair(refs[:pieces], 9 * pad, pad, 1), NT).astype(BF16)
    rows = mm(by_slot, placed(feature_ref[...], width), NT).astype(BF16)

    allowed = allowed_pairs(key_seg_ref[...], query_seg_ref[...], row_count)
    joined = stacked(refs[pieces : pieces + blocks])
    spread_heads(query_ref[...], query_heads)
    spread_heads(rows, row_heads)
    spread_heads(joined, key_heads)
    spread_heads(joined, value_heads, KVH)

    def one_group(group):
        keys, values = key_heads[group], value_heads[group]
        key_sum, value_sum = None, None
        for member in range(GROUP):
            head = group * GROUP + member
            head_query, head_rows = query_heads[head], row_heads[head]
            scores = jnp.where(allowed, mm(keys, head_query, NT) * SCALE, MASKED_SCORE)
            exact = jnp.exp(scores - lse_ref[head])
            dp = mm(values, head_rows, NT)
            weighted = exact * dp
            delta = jnp.sum(weighted, axis=0, keepdims=True)
            score_rows = (weighted - exact * delta).astype(BF16)
            query_sums[head] = mm(score_rows, keys, TN) * SCALE
            key_term = mm(score_rows, head_query)
            value_term = mm(exact.astype(BF16), head_rows)
            key_sum = key_term if key_sum is None else key_sum + key_term
            value_sum = value_term if value_sum is None else value_sum + value_term
        key_sums[group] = key_sum * SCALE
        value_sums[group] = value_sum

    for group in range(KVH):
        one_group(group)
    joined_sum = jnp.concatenate([gathered_heads(key_sums), gathered_heads(value_sums)], axis=1)
    for index, ref in enumerate(block_outs):
        ref[...] = joined_sum[index * row_count : (index + 1) * row_count].astype(ref.dtype)
    query_sum = gathered_heads(query_sums)
    query_out[...] = turn_lanes(query_sum, cos_ref[...], -sin_ref[...]).astype(BF16)


def canonical(value, place):
    high = value.astype(BF16)
    low = (value - high.astype(F32)).astype(BF16)
    return mm(high, place, NT) + mm(low, place, NT)


def qo_grads_body(pad, act_ref, act_output_ref, query_ref, rows_ref, *refs):
    sent_out, query_kept, output_kept, back_out = refs[-4:]
    half = act_ref.shape[1] // 2
    lefts = ((act_ref[...], query_ref[...]), (act_output_ref[...], rows_ref[...]))
    sent = [mm(act[:, half:], rows, TN) for act, rows in lefts]
    for slot in range(half // pad):
        part = slice(slot * pad, (slot + 1) * pad)
        store_pair(sent_out, slot * 9 * pad, pad, sent[0][part], sent[1][part])
    for (act, rows), out in zip(lefts, (query_kept, output_kept)):
        out[...] = mm(act[:, :half], rows, TN)
    back_out[...] = mm(query_ref[...], load_pair(refs[:-4], 9 * pad, pad, 0), NT)


def kv_grads_body(shard, pad, pieces, blocks, act_ref, feature_ref, owner_ref, cos_ref, sin_ref,
                  back_ref, tok_ref, middle_grad_ref, gains_ref, second_gain_ref, *refs):
    weights = stacked(refs[:pieces])
    parts = refs[pieces : pieces + blocks]
    sent_out, kept_out, grad_out = refs[pieces + blocks :]
    width = tok_ref.shape[1]
    total = parts[0][...]
    for part in parts[1:]:
        total = total + part[...].astype(F32)
    turned = turn_lanes(total, cos_ref[...], -sin_ref[...])
    lane = lax.broadcasted_iota(jnp.int32, total.shape, 1)
    rows = jnp.where(lane < KVW, turned, total).astype(BF16)
    back = canonical(back_ref[...] + mm(rows, weights, NT), placed(feature_ref[...], width))
    source = tok_ref[...].astype(F32)
    inverse = inverse_norm(source)
    normed = source * inverse
    first_gain = jnp.sum(back * normed, axis=0, keepdims=True)
    slots = owner_ref.shape[0]
    spread = spread_lanes(shard, 2 * KVW, width)
    mine = owner_ref[...] == lax.broadcasted_iota(jnp.int32, (slots, width), 1) // shard
    place_at = lax.broadcasted_iota(jnp.int32, (slots, slots * pad), 1)
    slot_at = lax.broadcasted_iota(jnp.int32, (slots, slots * pad), 0)
    extra = None
    for index, gain in enumerate((first_gain, second_gain_ref[0:1, :])):
        by_slot = mm(jnp.where(mine, gain, 0.0).astype(BF16), spread, NT).astype(BF16)
        pick = jnp.where(place_at == slot_at * pad + shard + index, 1.0, 0.0).astype(BF16)
        term = mm(pick, by_slot, TN)
        extra = term if extra is None else extra + term
    grads = mm(act_ref[...], rows, TN) + extra
    half = grads.shape[0] // 2
    sent_out[...] = grads[half:].astype(BF16)
    kept_out[...] = grads[:half]
    scaled = back * gains_ref[0:1, :]
    input_grad = middle_grad_ref[...] + inverse * (
        scaled - normed * jnp.mean(scaled * normed, axis=-1, keepdims=True)
    )
    grad_out[...] = jnp.transpose(input_grad)


def core_sum_body(pad, query_ref, output_ref, qo_got, kv_ref, kv_got, sent_out, query_out,
                  output_out, kv_out):
    query = query_ref[...] + load_pair([qo_got], 9 * pad, pad, 0).astype(F32)
    output = output_ref[...] + load_pair([qo_got], 9 * pad, pad, 1).astype(F32)
    kv = kv_ref[...] + kv_got[...].astype(F32)
    half = query.shape[0] // 2
    query_out[...] = query[:half]
    output_out[...] = output[:half]
    kv_out[...] = kv[:half]
    for slot in range(half // pad):
        part = slice(half + slot * pad, half + (slot + 1) * pad)
        store_pair(sent_out, slot * 12 * pad, pad, query[part], output[part])
        store_three(sent_out, slot * 12 * pad + 9 * pad, pad, kv[part])


def x_sum_body(pad, query_ref, output_ref, kv_ref, got_ref, *outs):
    query = query_ref[...] + load_pair([got_ref], 12 * pad, pad, 0).astype(F32)
    output = output_ref[...] + load_pair([got_ref], 12 * pad, pad, 1).astype(F32)
    kv = kv_ref[...] + load_three([got_ref], 12 * pad, 9 * pad, pad).astype(F32)
    for slot, out in enumerate(outs):
        part = slice(slot * pad, (slot + 1) * pad)
        store_pair(out, 0, pad, query[part], output[part])
        store_three(out, 9 * pad, pad, kv[part])


def feed_sum_body(hidden, kinds, kept_ref, got_ref, *outs):
    size = packed_rows(hidden)
    for slot, out in enumerate(outs):
        for kind in range(kinds):
            at = slot * kinds + kind
            got = load_packed([got_ref.at[pl.ds(at * size, size), :]], size, 0, hidden)
            total = kept_ref[at * hidden : (at + 1) * hidden, :] + got.astype(F32)
            store_packed(out, kind * size, total)


def totals_body(count, *refs):
    out = refs[-1]
    rows = refs[0].shape[0]
    for index in range(2):
        parts = refs[index * count : (index + 1) * count]
        total = parts[0][...]
        for ref in parts[1:]:
            total = total + ref[...].astype(F32)
        out[index * rows : (index + 1) * rows, :] = total.astype(BF16)


def total_body(*refs):
    total = refs[0][...]
    for ref in refs[1:-1]:
        total = total + ref[...].astype(F32)
    refs[-1][...] = total.astype(BF16)


def copies_total(shard, pad, hidden, first, both_refs, rest_refs):
    size = packed_rows(hidden)
    down = two_copies_packed(both_refs, 2 * size, 0, hidden)
    own, got = [load_packed([ref], 2 * size, size, hidden).astype(F32) for ref in both_refs]
    gate, up = jnp.where(first, own, got), jnp.where(first, got, own)
    query = sum(load_pair([ref], 12 * pad, pad, 0).astype(F32) for ref in rest_refs)
    output = sum(load_pair([ref], 12 * pad, pad, 1).astype(F32) for ref in rest_refs)
    kv = sum(load_three([ref], 12 * pad, 9 * pad, pad).astype(F32) for ref in rest_refs)
    return (
        query[:shard],
        kv[:shard, :KVW],
        kv[:shard, KVW:],
        output[:shard],
        gate,
        up,
        down,
        kv[shard : shard + 2, :shard],
    )


def two_copies_packed(refs, slot_rows, base, rows):
    return sum(load_packed([ref], slot_rows, base, rows).astype(F32) for ref in refs)


def moment_messages_body(shard, pad, hidden, stride, at_ref, both_ref, both_got,
                         rest_ref, rest_got, query_ref, key_ref, value_ref, output_ref, gate_ref,
                         up_ref, down_moment_ref, *refs):
    outs, scratch = refs[:-1], refs[-1]
    scratch[...] = jnp.zeros(scratch.shape, BF16)
    totals = copies_total(
        shard,
        pad,
        hidden,
        at_ref[2] == 0,
        (both_ref, both_got),
        (rest_ref, rest_got),
    )
    moments = [
        MOMENTUM * ref[...] + total
        for ref, total in zip(
            (query_ref, key_ref, value_ref, output_ref, gate_ref, up_ref, down_moment_ref), totals
        )
    ]
    for group, value in enumerate(moments[4:]):
        store_packed(scratch.at[group], 0, value)
    target = scratch.at[3]
    for which, value in enumerate((moments[0], moments[3])):
        for index in range(FULL):
            at = (which * FULL + index) * pad
            target[at : at + shard, :] = value[:, index * 128 : (index + 1) * 128].astype(BF16)
        at = 2 * FULL * pad
        target[at : at + shard, which * 64 : which * 64 + 64] = value[:, FULL * 128 :].astype(BF16)
    kv = jnp.concatenate([moments[1], moments[2]], axis=1)
    for index in range(3):
        at = (9 + index) * pad
        target[at : at + shard, :] = kv[:, index * 128 : (index + 1) * 128].astype(BF16)
    for other, out in enumerate(outs):
        out[...] = scratch[(at_ref[0] ^ other) // stride]


def moments_body(shard, pad, hidden, at_ref, both_ref, both_got, rest_ref, rest_got,
                 middle_ref, result_ref, result_got, *refs):
    moments, grads, news, out_tokens = refs[:8], refs[8:16], refs[16:24], refs[24]
    totals = copies_total(
        shard,
        pad,
        hidden,
        at_ref[2] == 0,
        (both_ref, both_got),
        (rest_ref, rest_got),
    )
    for moment, total, grad, new in zip(moments, totals, grads, news):
        grad[...] = total
        new[...] = MOMENTUM * moment[...] + total
    result = middle_ref[...] + result_ref[...] + result_got[...].astype(F32)
    out_tokens[...] = jnp.transpose(result).astype(BF16)


def self_product(left, out_ref):
    size = left.shape[0]
    for start in range(0, size, 256):
        end = min(start + 256, size)
        block = mm(left[start:], left[start:end], NT)
        out_ref[start:, start:end] = block
        if end < size:
            out_ref[start:end, end:] = jnp.transpose(block[end - start :])


def polar_steps(wide_ref, gram_ref, needed):
    size = wide_ref.shape[0]
    first = wide_ref[...]
    norm = jnp.sqrt(jnp.sum(first * first)) + NORM_FLOOR
    wide_ref[...] = first / norm

    def step(columns):
        row = lax.broadcasted_iota(jnp.int32, (size, size), 0)
        col = lax.broadcasted_iota(jnp.int32, (size, size), 1)
        diagonal = row == col
        rounded = wide_ref[...].astype(BF16)
        self_product(rounded, gram_ref)
        gram = gram_ref[...]
        mean = jnp.sum(jnp.where(diagonal, gram, 0.0)) / size
        rest = gram - jnp.where(diagonal, mean, 0.0)
        self_product(rest.astype(BF16), gram_ref)
        square = gram_ref[...] + (2.0 * mean) * rest
        square = square + jnp.where(diagonal, mean * mean, 0.0)
        poly = CUBIC_TERM * gram + QUINTIC_TERM * square
        shift = jnp.sum(jnp.where(diagonal, poly, 0.0)) / size
        poly_rest = (poly - jnp.where(diagonal, shift, 0.0)).astype(BF16)
        wide_ref[:, :columns] = (LINEAR_TERM + shift) * wide_ref[:, :columns] + mm(
            poly_rest, rounded[:, :columns]
        )

    def middle_step(index, carry):
        step(wide_ref.shape[1])
        return carry

    whole = needed == wide_ref.shape[1]
    lax.fori_loop(0, NS_STEPS if whole else NS_STEPS - 1, middle_step, 0)
    if not whole:
        step(needed)


def polar_body(pad, hidden, stride, slot_rows, pieces, at_ref, *refs):
    last = at_ref[0] // stride == 3

    @pl.when(last)
    def _():
        small_body(pad, slot_rows, pieces, at_ref, *refs)

    @pl.when(jnp.logical_not(last))
    def _():
        big_body(hidden, slot_rows, pieces, *refs)


def big_body(hidden, slot_rows, pieces, *refs):
    outs, wide_ref, gram_ref = refs[pieces:-4], refs[-4], refs[-2]
    tall = load_packed(refs[:pieces], slot_rows, 0, hidden)
    wide_ref[...] = jnp.transpose(tall.astype(F32))
    polar_steps(wide_ref, gram_ref, len(outs) * hidden)
    result = jnp.transpose(wide_ref[:, : len(outs) * hidden])
    for slot, out in enumerate(outs):
        if packed_rows(hidden) < out.shape[0]:
            out[...] = jnp.zeros(out.shape, BF16)
        store_packed(out, 0, result[slot * hidden : (slot + 1) * hidden])


def small_body(pad, slot_rows, pieces, at_ref, *refs):
    outs, large_ref, little_ref, gram_ref, little_gram_ref = refs[pieces:-4], *refs[-4:]
    ins = refs[:pieces]
    core = at_ref[1]
    large = jnp.where(
        core == 0,
        load_pair(ins, slot_rows, pad, 0).astype(F32),
        load_pair(ins, slot_rows, pad, 1).astype(F32),
    )
    little = load_three(ins, slot_rows, 9 * pad, pad).astype(F32)
    little = jnp.where(core == 0, little[:, :KVW], little[:, KVW : 2 * KVW])
    count = large.shape[0]
    large_ref[:, :count] = jnp.transpose(large)
    little_ref[...] = jnp.transpose(little)
    polar_steps(large_ref.at[:, :count], gram_ref, count)
    polar_steps(little_ref, little_gram_ref, count)
    large = jnp.transpose(large_ref[:, :count])
    little = jnp.transpose(little_ref[...])
    other = count // 2
    for slot, out in enumerate(outs):
        if 12 * pad < out.shape[0]:
            out[...] = jnp.zeros(out.shape, BF16)
        own = slice(slot * pad, (slot + 1) * pad)
        cross = slice(other + slot * pad, other + (slot + 1) * pad)
        store_pair(out, 0, pad, large[own], large[cross])
        store_three(
            out, 9 * pad, pad, jnp.concatenate([little[own], little[cross]], axis=1)
        )


def weights_body(shard, pad, hidden, stride, factors, at_ref, *refs):
    count = (len(refs) - 2 - 1 - 8 - 16) // 2
    answers, crosses = refs[:count], refs[count : 2 * count]
    gain_moment_ref = refs[2 * count]
    at = 2 * count + 1
    masters = refs[at : at + 8]
    news, rounded = refs[at + 8 : at + 16], refs[at + 16 : at + 24]
    scratch, cross_ref = refs[-2:]
    for other, ref in enumerate(crosses):

        @pl.when(at_ref[0] ^ other == 3 * stride)
        def _():
            cross_ref[...] = ref[...]

    for group in range(4):
        for other, ref in enumerate(answers):

            @pl.when(at_ref[0] ^ other == group * stride)
            def _():
                scratch[group] = ref[...]

    core = at_ref[1]
    target = scratch.at[3]
    rows = target.shape[0]
    own_large = load_pair([target], rows, pad, 0)[:shard].astype(F32)
    other_large = load_pair([cross_ref], rows, pad, 1)[:shard].astype(F32)
    own_little = load_three([target], rows, 9 * pad, pad)[:shard, :KVW].astype(F32)
    other_little = load_three([cross_ref], rows, 9 * pad, pad)[:shard, KVW:].astype(F32)
    first = core == 0
    polars = (
        jnp.where(first, own_large, other_large),
        jnp.where(first, own_little, other_little),
        jnp.where(first, other_little, own_little),
        jnp.where(first, other_large, own_large),
    ) + tuple(
        load_packed([scratch.at[group]], rows, 0, hidden).astype(F32) for group in range(3)
    )
    for master, polar, factor, new, low in zip(masters, polars, factors, news, rounded):
        weight = master[...] - factor * polar
        new[...] = weight
        low[...] = weight.astype(BF16)
    weight = masters[7][...] - GAIN_RATE * gain_moment_ref[...]
    news[7][...] = weight
    rounded[7][...] = weight.astype(BF16)


def local(
    tokens,
    out_grad,
    segments,
    query_copy,
    key_copy,
    value_copy,
    output_copy,
    gate_copy,
    up_copy,
    down_copy,
    gains_copy,
    query_master,
    key_master,
    value_master,
    output_master,
    gate_master,
    up_master,
    down_master,
    gains_master,
    query_moment,
    key_moment,
    value_moment,
    output_moment,
    gate_moment,
    up_moment,
    down_moment,
    gains_moment,
):
    x_size, z_size = lax.axis_size("x"), lax.axis_size("ctx")
    x_at, core_at, z_at = lax.axis_index("x"), lax.axis_index("core"), lax.axis_index("ctx")
    if z_size % 4:
        raise ValueError("ctx size")
    stride = z_size // 4
    slots = 2 * x_size * z_size
    rows, width = tokens.shape[1], tokens.shape[2]
    shard = query_copy.shape[0]
    pad = -(-(shard + 2) // 8) * 8
    hidden = down_copy.shape[0]
    back_blocks = z_size // 2
    blocks = back_blocks + 1
    at = jnp.stack([z_at, core_at, lax.axis_index("rep"), x_at]).astype(jnp.int32)
    bind = functools.partial

    def join(parts):
        total = sum(part.shape[0] for part in parts)
        return call(join_body, shaped(parts[0].dtype, total, parts[0].shape[1]), *parts)

    def on_column(value):
        return [value] + [flip(value, "ctx", other) for other in range(1, z_size)]

    def along_ctx(value):
        return join(on_column(value))

    def along_x(pieces):
        for bit in bits_of(x_size):
            pieces = pieces + [flip(piece, "x", bit) for piece in pieces]
        return pieces

    def along_core(pieces):
        return pieces + [flip(piece, "core", 1) for piece in pieces]

    kv_message = call(
        bind(kv_message_body, shard), shaped(BF16, pad, 2 * KVW), key_copy, value_copy, gains_copy,
    )
    kv_joined = along_ctx(kv_message)
    frequency = np.float32(ROPE_BASE) ** (
        np.float32(-2.0) * (np.arange(128) % (HD // 2)).astype(np.float32) / np.float32(HD)
    )
    tok, grad, cosine, sine, key_seg, query_seg, feature, owner = call(
        bind(setup_body, blocks, shard, pad, x_size, z_size),
        (
            shaped(BF16, rows, width),
            shaped(BF16, rows, width),
            shaped(F32, rows, 128),
            shaped(F32, rows, 128),
            shaped(F32, blocks * rows, 1),
            shaped(F32, 1, rows),
            shaped(jnp.int32, 1, slots * pad),
            shaped(jnp.int32, slots, 1),
        ),
        at,
        tokens[0].T,
        out_grad[0].T,
        segments,
        jnp.asarray(frequency[None, :], F32),
        scalars=1,
    )
    qo_message = call(
        bind(qo_message_body, shard, pad), shaped(BF16, 9 * pad, 128), query_copy, output_copy
    )
    size = packed_rows(hidden)
    feed_shard = jnp.where(lax.axis_index("rep") == 0, gate_copy.T, up_copy.T)
    kv_pieces = along_core(along_x([kv_joined]))
    qo_pieces = along_core(along_x([along_ctx(qo_message)]))
    other_grad = flip(grad, "core", 1)
    pieces = len(kv_pieces)

    kv_own, _, act_slots, gains = call(
        bind(kv_body, shard, pad, pieces),
        (
            shaped(BF16, rows, 2 * KVW),
            shaped(BF16, rows, width),
            shaped(BF16, rows, slots * pad),
            shaped(F32, 8, width),
        ),
        tok,
        feature,
        owner,
        cosine,
        sine,
        *kv_pieces,
    )
    kv_blocks = [kv_own]
    following = [(i, i + 1) for i in range(z_size - 1)]
    for _ in range(1, blocks):
        kv_blocks.append(lax.ppermute(kv_blocks[-1], "ctx", following))
    packed = shaped(BF16, z_size * size, 128)
    mine = call(pack_body, packed, *on_column(feed_shard))
    down = call(pack_body, packed, *on_column(down_copy))
    mine_pieces = along_x([mine])
    copied_pieces = [flip(piece, "rep", 1) for piece in mine_pieces]
    down_pieces = along_x([down])
    feed_pieces = len(down_pieces)
    queries = call(
        bind(query_body, pad), shaped(BF16, rows, width), act_slots, cosine, sine, *qo_pieces,
    )
    lse, act_output, middle, act_second = call(
        bind(attend_body, pad, pieces, blocks),
        (
            shaped(F32, H, 1, rows),
            shaped(BF16, rows, slots * pad),
            shaped(F32, rows, width),
            shaped(BF16, rows, width),
        ),
        queries,
        key_seg,
        query_seg,
        feature,
        tok,
        gains,
        *qo_pieces,
        *kv_blocks,
        scratch=[
            pltpu.VMEM((H, rows, HD), BF16),
            pltpu.VMEM((KVH, blocks * rows, HD), BF16),
            pltpu.VMEM((KVH, blocks * rows, HD), BF16),
            pltpu.VMEM((H, rows, HD), BF16),
        ],
    )

    other_act = flip(act_second, "core", 1)
    inner = slots // 2 * hidden
    hidden_rows, gate_rows, up_rows, second_own, second_send = call(
        bind(feed_body, hidden, feed_pieces),
        (shaped(BF16, 2 * rows, inner),) * 3
        + (shaped(F32, rows, width), shaped(BF16, rows, width)),
        at,
        act_second,
        other_act,
        grad,
        other_grad,
        *mine_pieces,
        *copied_pieces,
        *down_pieces,
        scalars=1,
    )
    second_got = flip(second_send, "core", 1)
    kept_slots = slots // 4

    def feed_gradients(lefts, rights):
        kinds = len(lefts)
        sent, kept = call(
            bind(feed_grads_body, hidden, kinds),
            (
                shaped(BF16, kept_slots * kinds * size, 128),
                shaped(F32, kept_slots * kinds * hidden, width),
            ),
            *lefts,
            *rights,
        )
        return sent, kept, flip(sent, "x", 1)

    def feed_totals(kinds, kept, got):
        parts = call(
            bind(feed_sum_body, hidden, kinds),
            (shaped(F32, kinds * size, 128),)
            + (shaped(BF16, kinds * size, 128),) * (z_size - 1),
            kept,
            got,
        )
        return [parts[0]] + [flip(parts[other], "ctx", other) for other in range(1, z_size)]

    def added(parts):
        total = call(total_body, shaped(BF16, *parts[0].shape), *parts)
        return total, flip(total, "rep", 1)

    _, down_kept, down_got = feed_gradients([hidden_rows], [grad, other_grad])
    pair_sent, pair_kept = call(
        bind(pair_grads_body, hidden),
        (shaped(BF16, slots // 2 * size, 128), shaped(F32, slots // 2 * hidden, width)),
        at,
        gate_rows,
        up_rows,
        act_second,
        other_act,
        scalars=1,
    )
    pair_got = flip(pair_sent, "rep", 1)
    feed_sent, feed_kept = call(
        bind(pair_sum_body, hidden),
        (shaped(BF16, kept_slots * size, 128), shaped(F32, kept_slots * hidden, width)),
        pair_kept,
        pair_got,
    )
    feed_got = flip(feed_sent, "x", 1)

    outs = call(
        bind(attend_back_body, pad, pieces, blocks),
        (
            shaped(BF16, rows, width),
            shaped(BF16, rows, width),
            shaped(F32, rows, width),
            shaped(F32, 8, width),
            shaped(F32, rows, 2 * KVW),
        )
        + (shaped(BF16, rows, 2 * KVW),) * back_blocks,
        second_own,
        second_got,
        middle,
        grad,
        gains,
        queries,
        key_seg,
        query_seg,
        feature,
        lse,
        cosine,
        sine,
        *qo_pieces,
        *kv_blocks,
        scratch=[
            pltpu.VMEM((H, rows, HD), BF16),
            pltpu.VMEM((H, rows, HD), BF16),
            pltpu.VMEM((KVH, blocks * rows, HD), BF16),
            pltpu.VMEM((KVH, blocks * rows, HD), BF16),
            pltpu.VMEM((H, rows, HD), F32),
            pltpu.VMEM((KVH, blocks * rows, HD), F32),
            pltpu.VMEM((KVH, blocks * rows, HD), F32),
        ],
    )
    query_rows, attn_rows, middle_grad, second_gain = outs[:4]
    kv_terms = [outs[4]]
    for back in range(1, blocks):
        pairs = [(i + back, i) for i in range(z_size - back)]
        kv_terms.append(lax.ppermute(outs[4 + back], "ctx", pairs))
    down_parts = feed_totals(1, down_kept, down_got)

    qo_sent, query_kept, output_kept, query_back = call(
        bind(qo_grads_body, pad),
        (
            shaped(BF16, slots // 2 * 9 * pad, 128),
            shaped(F32, slots // 2 * pad, width),
            shaped(F32, slots // 2 * pad, width),
            shaped(F32, rows, slots * pad),
        ),
        act_slots,
        act_output,
        query_rows,
        attn_rows,
        *qo_pieces,
    )
    qo_got = flip(qo_sent, "core", 1)
    kv_sent, kv_kept, input_grad = call(
        bind(kv_grads_body, shard, pad, pieces, blocks),
        (
            shaped(BF16, slots // 2 * pad, 2 * KVW),
            shaped(F32, slots // 2 * pad, 2 * KVW),
            shaped(F32, width, rows),
        ),
        act_slots,
        feature,
        owner,
        cosine,
        sine,
        query_back,
        tok,
        middle_grad,
        gains,
        second_gain,
        *kv_pieces,
        *kv_terms,
    )
    kv_got = flip(kv_sent, "core", 1)
    feed_parts = feed_totals(1, feed_kept, feed_got)
    rest_sent, query_kept, output_kept, kv_kept = call(
        bind(core_sum_body, pad),
        (
            shaped(BF16, kept_slots * 12 * pad, 128),
            shaped(F32, kept_slots * pad, width),
            shaped(F32, kept_slots * pad, width),
            shaped(F32, kept_slots * pad, 2 * KVW),
        ),
        query_kept,
        output_kept,
        qo_got,
        kv_kept,
        kv_got,
    )
    rest_got = flip(rest_sent, "x", 1)
    rest_parts = call(
        bind(x_sum_body, pad),
        (shaped(F32, 12 * pad, 128),) + (shaped(BF16, 12 * pad, 128),) * (z_size - 1),
        query_kept,
        output_kept,
        kv_kept,
        rest_got,
    )
    rest_parts = [rest_parts[0]] + [
        flip(rest_parts[other], "ctx", other) for other in range(1, z_size)
    ]
    both_total = call(
        bind(totals_body, z_size), shaped(BF16, 2 * size, 128), *down_parts, *feed_parts
    )
    both_copied = flip(both_total, "rep", 1)
    rest_total, rest_copied = added(rest_parts)

    slot_rows = max(size, 12 * pad)
    message = shaped(BF16, slot_rows, 128)
    sums = (both_total, both_copied, rest_total, rest_copied)
    natural = (
        query_moment,
        key_moment,
        value_moment,
        output_moment,
        gate_moment.T,
        up_moment.T,
        down_moment,
        gains_moment,
    )
    messages = call(
        bind(moment_messages_body, shard, pad, hidden, stride),
        (message,) * z_size,
        at,
        *sums,
        *natural[:7],
        scratch=[pltpu.VMEM((4, slot_rows, 128), BF16)],
        scalars=1,
    )
    owner_columns = [g * stride for g in range(4)]
    arrived = [messages[0]]
    for other in range(1, z_size):
        pairs = [(d ^ other, d) for d in owner_columns]
        arrived.append(lax.ppermute(messages[other], "ctx", pairs))
    matrix_pieces = along_core(along_x([join(arrived)]))
    result_own, result_send = call(
        bind(result_body, hidden),
        (shaped(F32, rows, width), shaped(BF16, rows, width)),
        hidden_rows,
        *down_pieces,
    )
    result_got = flip(result_send, "core", 1)
    moment_types = tuple(shaped(F32, *value.shape) for value in natural)
    outs = call(
        bind(moments_body, shard, pad, hidden),
        moment_types * 2 + (shaped(BF16, width, rows),),
        at,
        *sums,
        middle,
        result_own,
        result_got,
        *natural,
        scalars=1,
    )
    totals, new_moments, out_tokens = list(outs[:8]), list(outs[8:16]), outs[16]

    large_lanes = max(hidden, pad) * slots

    solved = call(
        bind(polar_body, pad, hidden, stride, slot_rows, pieces),
        (message,) * z_size,
        at,
        *matrix_pieces,
        scratch=[
            pltpu.VMEM((width, large_lanes), F32),
            pltpu.VMEM((KVW, slots * pad), F32),
            pltpu.VMEM((width, width), F32),
            pltpu.VMEM((KVW, KVW), F32),
        ],
        scalars=1,
    )
    answers = [solved[0]]
    for other in range(1, z_size):
        pairs = [(d, d ^ other) for d in owner_columns]
        answers.append(lax.ppermute(solved[other], "ctx", pairs))
    crossed = [flip(answer, "core", 1) for answer in answers]
    masters = (
        query_master,
        key_master,
        value_master,
        output_master,
        gate_master.T,
        up_master.T,
        down_master,
        gains_master,
    )
    full = slots * hidden
    full_shapes = (
        (width, width),
        (width, KVW),
        (width, KVW),
        (width, width),
        (width, full),
        (width, full),
        (full, width),
    )
    factors = [STEP_SIZE * math.sqrt(max(shape) / shape[0]) for shape in full_shapes]
    outs = call(
        bind(weights_body, shard, pad, hidden, stride, factors),
        tuple(shaped(F32, *value.shape) for value in masters)
        + tuple(shaped(BF16, *value.shape) for value in masters),
        at,
        *answers,
        *crossed,
        new_moments[7],
        *masters,
        scratch=[pltpu.VMEM((4, slot_rows, 128), BF16), pltpu.VMEM((slot_rows, 128), BF16)],
        scalars=1,
    )
    weights, rounded = list(outs[:8]), list(outs[8:])
    for values in (totals, new_moments, weights, rounded):
        for index in (4, 5):
            values[index] = values[index].T
    return (out_tokens.T[None], input_grad.T[None], *totals, *new_moments, *weights, *rounded)


def solution(mesh):
    dp_size, ctx_size, rep_size = (mesh.shape[name] for name in ("dp", "ctx", "rep"))
    split = Mesh(
        mesh.devices.reshape(dp_size // 2, 2, ctx_size, rep_size), ("x", "core", "ctx", "rep")
    )
    batch = ("x", "core", "rep")
    parts = ("x", "core", "ctx")
    by_row, by_column = P(parts, None), P(None, parts)
    weights = (by_row, by_row, by_row, by_row, by_column, by_column, by_row, by_column)
    token_spec = P(batch, "ctx", None)

    return jax.shard_map(
        local,
        mesh=split,
        in_specs=(token_spec, token_spec, P(batch, None)) + weights * 3,
        out_specs=(token_spec, token_spec) + weights * 4,
        check_vma=False,
    )
```
